32 devices in a mesh: row: 2 (over x), col: 4 (over y, core), rhs: 4 (over z).
Axes of the slice: x: 2, y: 2, z: 4, core: 2. Of those that a mesh axis runs over, the one named last changes fastest.
Arguments:
- right_side: float32 [2, 64, 8192], P('row', 'rhs', 'col'), may hold values from -6 to 6
- guess: float32 [2, 64, 8192], P('row', 'rhs', 'col'), may hold values from -6 to 6
- inverse: bfloat16 [2, 8192, 8192], P('row', 'rhs', 'col'), may hold values from -0.0625 to 0.0625
- left_factor: bfloat16 [2, 2, 64, 8192], P('row', None, None, 'col'), may hold values from -0.5 to 0.5
- right_factor: bfloat16 [2, 2, 64, 8192], P('row', None, None, 'col'), may hold values from -0.0625 to 0.0625
- ranks: int32 [2, 2], replicated, may hold values from 16 to 64
Outputs:
- solution: float32 [2, 64, 8192], P('row', 'rhs', 'col')
The draws below stay inside these ranges and needn't reach their ends.
Inputs may be any that keep to these rules, and one draw needn't show every extreme that they name: ranks[i, j] is the rank of the block in block row i and block column j; diagonal entries are not read.
All inputs are finite; a program needn't handle non-finite values.
Results may differ from the reference program's by a relative error of at most 0.008.
Values may be sent and summed in bfloat16 or wider, within the bound.
A program may use at most 128 MiB of HBM per device.

```python
import jax
import jax.numpy as jnp
from jax import lax

M = 8192
K = 64
R = 64
NB = 2


def place_ends(result, rng, low, high):
    longest = result.shape.index(max(result.shape))
    spots = []
    for shift in (0, 1):
        where = [jax.random.randint(jax.random.fold_in(rng, axis), (), 0, length) for axis, length in enumerate(result.shape)]
        where[longest] = (where[longest] + shift) % result.shape[longest]
        spots.append(tuple(where))
    return result.at[spots[0]].set(low).at[spots[1]].set(high)


def block_levels(key, dims, shards, smallest, top_value):
    level, own = 1.0, jax.random.fold_in(key, 6)
    for dim, blocks in shards:
        steps = jnp.exp(jax.random.uniform(jax.random.fold_in(own, dim), (blocks,), jnp.float32, smallest / len(shards), top_value / len(shards)))
        level = level * jnp.repeat(steps, dims[dim] // blocks).reshape([-1 if axis == dim else 1 for axis in range(len(dims))])
    return level


def noise(own_key, extent, spread, bound, cuts=(), kind=jnp.bfloat16):
    factor_of = block_levels(own_key, extent, cuts, -0.22, 0.18) if cuts else 1.0
    drawn = jax.random.normal(own_key, extent, jnp.float32) * spread * factor_of
    return jnp.minimum(jnp.maximum(drawn, -bound), bound).astype(kind)


def setup_inputs(seed: int = 0) -> dict:
    arg_keys = jax.random.split(jax.random.key(seed), 7)
    return {
        "right_side": noise(arg_keys[0], (NB, R, M), 1.0, 6.0, ((0, 2), (1, 4), (2, 4)), jnp.float32),
        "guess": noise(arg_keys[1], (NB, R, M), 1.0, 6.0, ((0, 2), (1, 4), (2, 4)), jnp.float32),
        "inverse": noise(arg_keys[2], (NB, M, M), M ** -0.5, 0.0625, ((0, 2), (1, 4), (2, 4))),
        "left_factor": noise(arg_keys[3], (NB, NB, K, M), (K * NB) ** -0.5, 0.5, ((0, 2), (3, 4))),
        "right_factor": noise(arg_keys[4], (NB, NB, K, M), M ** -0.5, 0.0625, ((0, 2), (3, 4))),
        "ranks": place_ends(jax.random.randint(arg_keys[5], (NB, NB), K // 4, K + 1), jax.random.fold_in(arg_keys[5], 1), K // 4, K).astype(jnp.int32),
    }


def reference(right_side, guess, inverse, left_factor, right_factor, ranks):
    keep = (jnp.arange(K, dtype=jnp.int32)[None, None, :] < ranks[:, :, None]).astype(jnp.float32)
    keep_swap = jnp.transpose(keep, (1, 0, 2))
    right_wide = right_factor.astype(jnp.float32)
    guess_low = lax.optimization_barrier(guess.astype(jnp.bfloat16)).astype(jnp.float32)
    old_coef = jnp.einsum("jrm,jikm->jirk", guess_low, right_wide, precision=lax.Precision.HIGHEST)
    old_coef = (old_coef * keep_swap[:, :, None, :]).astype(jnp.bfloat16)
    solved = []
    new_coef = []
    for t in range(NB):
        coupled = jnp.zeros((R, M), jnp.float32)
        for j in range(NB):
            if j > t:
                coupled = coupled + jnp.dot(old_coef[j, t], left_factor[t, j], preferred_element_type=jnp.float32)
            elif j < t:
                coupled = coupled + jnp.dot(new_coef[j][t], left_factor[t, j], preferred_element_type=jnp.float32)
        residue = (right_side[t] - coupled).astype(jnp.bfloat16)
        current = jnp.dot(residue, inverse[t], preferred_element_type=jnp.float32)
        solved.append(current)
        current_low = lax.optimization_barrier(current.astype(jnp.bfloat16)).astype(jnp.float32)
        coef = jnp.einsum("rm,ikm->irk", current_low, right_wide[t], precision=lax.Precision.HIGHEST)
        new_coef.append((coef * keep[:, t][:, None, :]).astype(jnp.bfloat16))
    return jnp.stack(solved)
```

```python
import functools

import jax
import jax.numpy as jnp
from jax import lax
from jax.experimental import pallas as pl
from jax.experimental.pallas import tpu as pltpu
from jax.sharding import PartitionSpec as P

F32 = jnp.float32
BF16 = jnp.bfloat16
TILE = 512
CHUNKS = 2


def dot(a, b):
    return lax.dot_general(a, b, (((1,), (0,)), ((), ())), preferred_element_type=F32)


def dot_t(a, b):
    return lax.dot_general(a, b, (((1,), (1,)), ((), ())), preferred_element_type=F32)


def fold(value):
    half = value.shape[0] // 2
    return jnp.concatenate([value[:half], value[half:]], axis=1)


def unfold(value):
    half = value.shape[1] // 2
    return jnp.concatenate([value[:, :half], value[:, half:]], axis=0)


def kernel(
    nb, nc, nz, width,
    rhs_ref, guess_ref, inv_ref, left_ref, right_ref, ranks_ref, out_ref,
    inv, rhs_v, guess_v, right_v, low, x, lf, p_rhs, p_left,
    a_out, a_in, a_own, a_sum, c_out, c_in, n_out, n_in, p_new, q_new,
    li_out, li_in, s_out, s_in, k_out, k_in, k_all, coef_v,
    inv_sem, in_sem, own_sem, x_send, x_recv, l_send, l_recv, ls_send, ls_recv, sib_send, sib_recv,
    a_send, a_recv, c_send, c_recv, n_send, n_recv, li_send, li_recv, rs_send, rs_recv, k_send, k_recv,
):
    row, col, z = lax.axis_index("row"), lax.axis_index("col"), lax.axis_index("rhs")
    slots, part = low.shape[1:]
    m = inv.shape[2]
    rows = nz * slots
    sub = m // nz
    half = col % 2
    sibling = (row, col + 1 - 2 * half, z)
    diag = col == z
    sent = []

    def remote(src, dst, send, recv, where):
        return pltpu.make_async_remote_copy(
            src_ref=src, dst_ref=dst, send_sem=send, recv_sem=recv,
            device_id=where, device_id_type=pl.DeviceIdType.MESH,
        )

    def start(pred, copy):
        @pl.when(pred)
        def _():
            copy.start()
        sent.append((pred, copy))

    around = [(dc, dz) for dz in range(nz) for dc in range(nc)]

    def there(r, dc, dz):
        return (r, lax.rem(col + dc, nc), lax.rem(z + dz, nz))

    barrier = pltpu.get_barrier_semaphore()
    for dc, dz in around[1:]:
        pl.semaphore_signal(barrier, inc=1, device_id=there(row, dc, dz), device_id_type=pl.DeviceIdType.MESH)
    for r in range(1, nb):
        @pl.when(row < r)
        def _():
            for dc, dz in around:
                pl.semaphore_signal(barrier, inc=1, device_id=there(r, dc, dz), device_id_type=pl.DeviceIdType.MESH)
    early = [
        pltpu.make_async_copy(src, dst, in_sem.at[i])
        for i, (src, dst) in enumerate(
            ((rhs_ref.at[0], rhs_v), (guess_ref.at[0], guess_v), (right_ref.at[0], right_v))
        )
    ]
    for load in early:
        load.start()
    ahead = jnp.where(row < nb - 1, 1 - half, half)
    loads = []
    for order in range(2):
        h = ahead if order == 0 else 1 - ahead
        load = pltpu.make_async_copy(
            inv_ref.at[0, pl.ds(pl.multiple_of(h * part, part), part)], inv.at[h], inv_sem.at[order]
        )
        load.start()
        loads.append(load)

    early[0].wait()
    for h in range(2):
        low[h] = rhs_v[:, h * part:(h + 1) * part].astype(BF16)
    early[1].wait()
    early[2].wait()

    @pl.when(row > 0)
    def _():
        coef = dot_t(guess_v[...].astype(BF16), right_v[...].reshape(nb * width, m))
        for i in range(nb - 1):
            c_out[i] = fold(coef[:, i * width:(i + 1) * width])

    pl.semaphore_wait(barrier, nc * nz - 1 + row * (nc * nz))

    for i in range(nb - 1):
        for k, (dc, dz) in enumerate(around):
            start(row > i, remote(c_out.at[i], c_in.at[row, col, z], c_send.at[i, k], c_recv.at[row, col, z], there(i, dc, dz)))

    mine = pl.ds(pl.multiple_of(z * slots, slots), slots)

    def send_x(pred):
        for c in range(nc):
            start(
                pred & jnp.logical_not(diag & (col == c)),
                remote(low.at[c % 2], x.at[c % 2, mine], x_send.at[c], x_recv.at[z], (row, c, col)),
            )

    def own(q):
        return pltpu.make_async_copy(
            left_ref.at[0, lax.rem(row + 1 + q, nb), :, pl.ds(pl.multiple_of(half * part, part), part)],
            lf.at[q, half], own_sem.at[q],
        )

    send_x(row == 0)
    for q in range(nb - 1):
        block = lax.rem(row + 1 + q, nb)
        for c in range(nc):
            start(
                diag & (col != c),
                remote(
                    left_ref.at[0, block, :, pl.ds((c % 2) * part, part)], lf.at[q, c % 2],
                    l_send.at[q, c], l_recv.at[q], (row, c, z),
                ),
            )
    send_x(row > 0)

    @pl.when(diag)
    def _():
        for q in range(nb - 1):
            own(q).start()
        x[half, mine] = low[half]

    def wait_left(q):
        @pl.when(diag)
        def _():
            own(q).wait()

        @pl.when(jnp.logical_not(diag))
        def _():
            spot = lf.at[q, half]
            remote(spot, spot, l_send.at[0, 0], l_recv.at[q], sibling).wait_recv()

    def wait_x():
        for zz in range(nz):
            @pl.when(jnp.logical_not(diag & (z == zz)))
            def _():
                spot = x.at[half, pl.ds(zz * slots, slots)]
                remote(spot, spot, x_send.at[0], x_recv.at[zz], sibling).wait_recv()

    def send_new(t, i):
        for k, (dc, dz) in enumerate(around):
            start(
                row == t,
                remote(n_out.at[i], n_in.at[t, col, z], n_send.at[i, k], n_recv.at[t, col, z], there(i, dc, dz)),
            )

    strip = part // 4
    for t in range(nb - 1):
        later = nb - 1 - t

        @pl.when(row == t)
        def _():
            span = pl.ds(0, later)
            swap = remote(a_out.at[span], a_in.at[span], a_send, a_recv, sibling)
            loads[0].wait()

            def theirs(i, _):
                cut = pl.ds(pl.multiple_of(i * strip, strip), strip)
                for b in range(later):
                    a_out[b, cut] = dot_t(inv[1 - half, cut], right_v[t + 1 + b]).astype(BF16)
                return _

            lax.fori_loop(0, part // strip, theirs, 0)
            swap.start()
            loads[1].wait()

            def ours(i, _):
                cut = pl.ds(pl.multiple_of(i * strip, strip), strip)
                for b in range(later):
                    a_own[b, cut] = dot_t(inv[half, cut], right_v[t + 1 + b])
                return _

            lax.fori_loop(0, part // strip, ours, 0)
            swap.wait()
            for b in range(later):
                a_sum[b] = (a_own[b] + a_in[b].astype(F32)).astype(BF16)

    def piece(t, zz):
        span = pl.ds(0, t * width)
        return remote(li_out.at[zz, span], li_in.at[z, span], li_send.at[zz], li_recv.at[z], (row, col, zz))

    for t in range(1, nb):
        later = nb - 1 - t
        tall = t * width

        @pl.when(row == t)
        def _():
            swaps = []
            for q in range(later, nb - 1):
                wait_left(q)
                spot = lf.at[q, half]
                copy = remote(spot, spot, ls_send.at[q], ls_recv.at[q], sibling)
                copy.start()
                swaps.append(copy)
            if not later:
                loads[0].wait()

            def first(i, _):
                cut = pl.ds(pl.multiple_of(i * TILE, TILE), TILE)
                p_left[:tall, cut] = dot(lf[later:, half].reshape(tall, part), inv[half, :, cut])
                return _

            lax.fori_loop(0, m // TILE, first, 0)
            if not later:
                loads[1].wait()
            for copy in swaps:
                copy.wait_recv()
            for zz in range(nz):
                cut = slice(zz * sub, (zz + 1) * sub)
                value = p_left[:tall, cut] + dot(lf[later:, 1 - half].reshape(tall, part), inv[1 - half, :, cut])
                li_out[zz, :tall] = value.astype(BF16)

                @pl.when(z != zz)
                def _():
                    piece(t, zz).start()

            for copy in swaps:
                copy.wait_send()

    swap = remote(x.at[half], x.at[half], sib_send, sib_recv, sibling)
    for t in range(nb):
        later = nb - 1 - t

        @pl.when(row == t)
        def _():
            if later:
                blocks = []
                for j in range(t + 1, nb):
                    parts = []
                    for zz in range(nz):
                        total = None
                        for c in range(nc):
                            spot = c_in.at[j, c, zz]
                            remote(spot, spot, c_send.at[0, 0], c_recv.at[j, c, zz], sibling).wait_recv()
                            term = c_in[j, c, zz]
                            total = term if total is None else total + term
                        parts.append(unfold(total))
                    whole = jnp.concatenate(parts, axis=0)
                    lane = lax.broadcasted_iota(jnp.int32, whole.shape, 1)
                    blocks.append(jnp.where(lane < ranks_ref[t, j], whole, jnp.zeros_like(whole)).astype(BF16))
                coefs = blocks[0] if later == 1 else jnp.concatenate(blocks, axis=1)
                for q in range(later):
                    wait_left(q)
            wait_x()
            if later:
                coupled = dot(coefs, lf[:later, half].reshape(later * width, part))
                rest = (x[half].astype(F32) - coupled).astype(BF16)
                x[half] = rest
            swap.start()
            if later:
                for i in range(t + 1, nb):
                    share = dot(rest, a_sum[i - t - 1])
                    if t:
                        p_new[i] = share
                        for j in range(t):
                            q_new[i, j] = dot(lf[later + j, half], a_sum[i - t - 1])
                    else:
                        n_out[i] = fold(share).astype(BF16)

    for i in range(1, nb):
        send_new(0, i)

    def first(i, _):
        cut = pl.ds(pl.multiple_of(i * TILE, TILE), TILE)
        p_rhs[:, cut] = dot(x[half], inv[half, :, cut])
        return _

    lax.fori_loop(0, m // TILE, first, 0)
    far = x.at[1 - half]
    remote(far, far, sib_send, sib_recv, sibling).wait_recv()

    span_m = m // CHUNKS
    others = [lax.rem(z + step, nz) for step in range(1, nz)]

    def pieces(ch):
        return [
            remote(
                s_out.at[ch, other], s_in.at[ch, z], rs_send.at[ch, i], rs_recv.at[ch, z], (row, col, other)
            )
            for i, other in enumerate(others)
        ]

    def across(i, other):
        return remote(k_out.at[other], k_in.at[z], k_send.at[i], k_recv.at[z], (row, col, other))

    for ch in range(CHUNKS):
        cut = slice(ch * span_m, (ch + 1) * span_m)
        now = p_rhs[:, cut] + dot(x[1 - half], inv[1 - half, :, cut])
        p_rhs[:, cut] = now
        for zz in range(nz):
            s_out[ch, zz] = now[zz * slots:(zz + 1) * slots].astype(BF16)
        for copy in pieces(ch):
            copy.start()
    swap.wait_send()

    for t in range(1, nb):
        later = nb - 1 - t
        tall = t * width

        @pl.when(row == t)
        def _():
            blocks = []
            for j in range(t):
                total = None
                for c in range(nc):
                    for zz in range(nz):
                        spot = n_in.at[j, c, zz]
                        remote(spot, spot, n_send.at[0, 0], n_recv.at[j, c, zz], sibling).wait_recv()
                        term = n_in[j, c, zz].astype(F32)
                        total = term if total is None else total + term
                whole = unfold(total)
                lane = lax.broadcasted_iota(jnp.int32, whole.shape, 1)
                blocks.append(jnp.where(lane < ranks_ref[t, j], whole, jnp.zeros_like(whole)).astype(BF16))
            for i in range(t + 1, nb):
                share = p_new[i]
                for j in range(t):
                    share = share - dot(blocks[j], q_new[i, j].astype(BF16))
                n_out[i] = fold(share).astype(BF16)
            coefs = blocks[0] if t == 1 else jnp.concatenate(blocks, axis=1)
            coef_v[:, :tall] = coefs

        for i in range(t + 1, nb):
            send_new(t, i)

        @pl.when(row == t)
        def _():
            for other in others:
                spot = li_in.at[other, pl.ds(0, tall)]
                remote(spot, spot, li_send.at[0], li_recv.at[other], sibling).wait_recv()
            total = li_out[z, :tall].astype(F32)
            for other in others:
                total = total + li_in[other, :tall].astype(F32)
            value = dot(coef_v[:, :tall], total.astype(BF16))
            for zz in range(nz):
                k_out[zz] = value[zz * slots:(zz + 1) * slots].astype(BF16)
            for i, other in enumerate(others):
                across(i, other).start()
            k_all[...] = value

    for ch in range(CHUNKS):
        cut = slice(ch * span_m, (ch + 1) * span_m)
        total = p_rhs[mine, cut]
        for other in others:
            spot = s_in.at[ch, other]
            remote(spot, spot, rs_send.at[0, 0], rs_recv.at[ch, other], (row, col, other)).wait_recv()
            total = total + s_in[ch, other].astype(F32)
        out_ref[0, :, cut] = total

    @pl.when(row > 0)
    def _():
        def take(where, value):
            cut = pl.ds(pl.multiple_of(where * sub, sub), sub)
            out_ref[0, :, cut] = out_ref[0, :, cut] - value

        take(z, k_all[mine])
        for i, other in enumerate(others):
            spot = k_in.at[other]
            remote(spot, spot, k_send.at[0], k_recv.at[other], (row, col, other)).wait_recv()
            take(other, k_in[other].astype(F32))
        for i, other in enumerate(others):
            across(i, other).wait_send()

    for t in range(1, nb):
        for zz in range(nz):
            @pl.when((row == t) & (z != zz))
            def _():
                piece(t, zz).wait_send()
    for ch in range(CHUNKS):
        for copy in pieces(ch):
            copy.wait_send()
    for pred, copy in sent:
        @pl.when(pred)
        def _():
            copy.wait_send()


def solution(mesh):
    nb, nc, nz = mesh.shape["row"], mesh.shape["col"], mesh.shape["rhs"]

    def body(right_side, guess, inverse, left_factor, right_factor, ranks):
        slots, m = right_side.shape[1:]
        width = left_factor.shape[2]
        rows = nz * slots
        part = inverse.shape[1] // 2
        pairs = nb - 1
        tall = pairs * width
        sub = m // nz
        dma = pltpu.SemaphoreType.DMA
        hbm = pl.BlockSpec(memory_space=pltpu.HBM)
        vmem = pl.BlockSpec(memory_space=pltpu.VMEM)
        return pl.pallas_call(
            functools.partial(kernel, nb, nc, nz, width),
            out_shape=jax.ShapeDtypeStruct(right_side.shape, F32),
            in_specs=[
                hbm, hbm, hbm, hbm, hbm,
                pl.BlockSpec(memory_space=pltpu.SMEM),
            ],
            out_specs=vmem,
            scratch_shapes=[
                pltpu.VMEM((2, part, m), BF16),
                pltpu.VMEM((slots, m), F32),
                pltpu.VMEM((slots, m), F32),
                pltpu.VMEM((nb, width, m), BF16),
                pltpu.VMEM((2, slots, part), BF16),
                pltpu.VMEM((2, rows, part), BF16),
                pltpu.VMEM((pairs, 2, width, part), BF16),
                pltpu.VMEM((rows, m), F32),
                pltpu.VMEM((tall, m), F32),
                pltpu.VMEM((pairs, part, width), BF16),
                pltpu.VMEM((pairs, part, width), BF16),
                pltpu.VMEM((pairs, part, width), F32),
                pltpu.VMEM((pairs, part, width), BF16),
                pltpu.VMEM((pairs, slots // 2, 2 * width), F32),
                pltpu.VMEM((nb, nc, nz, slots // 2, 2 * width), F32),
                pltpu.VMEM((nb, rows // 2, 2 * width), BF16),
                pltpu.VMEM((pairs, nc, nz, rows // 2, 2 * width), BF16),
                pltpu.VMEM((nb, rows, width), F32),
                pltpu.VMEM((nb, nb, width, width), F32),
                pltpu.VMEM((nz, tall, sub), BF16),
                pltpu.VMEM((nz, tall, sub), BF16),
                pltpu.VMEM((CHUNKS, nz, slots, m // CHUNKS), BF16),
                pltpu.VMEM((CHUNKS, nz, slots, m // CHUNKS), BF16),
                pltpu.VMEM((nz, slots, sub), BF16),
                pltpu.VMEM((nz, slots, sub), BF16),
                pltpu.VMEM((rows, sub), F32),
                pltpu.VMEM((rows, tall), BF16),
                dma((2,)), dma((3,)), dma((pairs,)),
                dma((nc,)), dma((nz,)),
                dma((pairs, nc)), dma((pairs,)),
                dma((pairs,)), dma((pairs,)),
                dma, dma,
                dma, dma,
                dma((pairs, nc * nz)), dma((nb, nc, nz)),
                dma((nb, nc * nz)), dma((pairs, nc, nz)),
                dma((nz,)), dma((nz,)),
                dma((CHUNKS, nz - 1)), dma((CHUNKS, nz)),
                dma((nz - 1,)), dma((nz,)),
            ],
            compiler_params=pltpu.CompilerParams(
                collective_id=0, has_side_effects=True, vmem_limit_bytes=60 * 1024 * 1024
            ),
        )(right_side, guess, inverse, left_factor, right_factor, ranks)

    in_specs = (
        P("row", "rhs", "col"),
        P("row", "rhs", "col"),
        P("row", "rhs", "col"),
        P("row", None, None, "col"),
        P("row", None, None, "col"),
        P(),
    )
    out_specs = P("row", "rhs", "col")
    return jax.shard_map(body, mesh=mesh, in_specs=in_specs, out_specs=out_specs, check_vma=False)
```

```python
import functools

import jax
import jax.numpy as jnp
from jax import lax
from jax.experimental import pallas as pl
from jax.experimental.pallas import tpu as pltpu
from jax.sharding import PartitionSpec as P

F32 = jnp.float32
BF16 = jnp.bfloat16
TILE = 512
CHUNKS = 2


def dot(a, b):
    return lax.dot_general(a, b, (((1,), (0,)), ((), ())), preferred_element_type=F32)


def dot_t(a, b):
    return lax.dot_general(a, b, (((1,), (1,)), ((), ())), preferred_element_type=F32)


def fold(value):
    half = value.shape[0] // 2
    return jnp.concatenate([value[:half], value[half:]], axis=1)


def unfold(value):
    half = value.shape[1] // 2
    return jnp.concatenate([value[:, :half], value[:, half:]], axis=0)


def kernel(
    nb, nc, nz, width,
    rhs_ref, guess_ref, inv_ref, left_ref, right_ref, ranks_hbm, out_ref,
    inv, rhs_v, guess_v, right_v, low, x, lf, p_rhs, p_left,
    a_out, a_in, a_own, a_sum, c_out, c_in, n_out, n_in, p_new, q_new,
    li_out, li_in, s_out, s_in, k_out, k_in, k_all, coef_v, li_sum, ranks_ref,
    inv_sem, in_sem, own_sem, x_send, x_recv, l_send, l_recv, ls_send, ls_recv, sib_send, sib_recv,
    a_send, a_recv, c_send, c_recv, n_send, n_recv, li_send, li_recv, rs_send, rs_recv, k_send, k_recv,
):
    row, col, z = lax.axis_index("row"), lax.axis_index("col"), lax.axis_index("rhs")
    slots, part = low.shape[1:]
    m = inv.shape[2]
    rows = nz * slots
    wide = m // 2
    half = col % 2
    sibling = (row, col + 1 - 2 * half, z)
    diag = col == z
    sent = []

    def remote(src, dst, send, recv, where):
        return pltpu.make_async_remote_copy(
            src_ref=src, dst_ref=dst, send_sem=send, recv_sem=recv,
            device_id=where, device_id_type=pl.DeviceIdType.MESH,
        )

    def start(pred, copy):
        @pl.when(pred)
        def _():
            copy.start()
        sent.append((pred, copy))

    around = [(dc, dz) for dz in range(nz) for dc in range(nc)]

    def there(r, dc, dz):
        return (r, lax.rem(col + dc, nc), lax.rem(z + dz, nz))

    barrier = pltpu.get_barrier_semaphore()
    for dc, dz in around[1:]:
        pl.semaphore_signal(barrier, inc=1, device_id=there(row, dc, dz), device_id_type=pl.DeviceIdType.MESH)
    for r in range(1, nb):
        @pl.when(row < r)
        def _():
            for dc, dz in around:
                pl.semaphore_signal(barrier, inc=1, device_id=there(r, dc, dz), device_id_type=pl.DeviceIdType.MESH)
    early = [
        pltpu.make_async_copy(src, dst, in_sem.at[i])
        for i, (src, dst) in enumerate(
            ((rhs_ref.at[0], rhs_v), (guess_ref.at[0], guess_v), (right_ref.at[0], right_v), (ranks_hbm, ranks_ref))
        )
    ]
    for load in early:
        load.start()
    ahead = jnp.where(row < nb - 1, 1 - half, half)
    loads = []
    for order in range(2):
        h = ahead if order == 0 else 1 - ahead
        load = pltpu.make_async_copy(
            inv_ref.at[0, pl.ds(pl.multiple_of(h * part, part), part)], inv.at[h], inv_sem.at[order]
        )
        load.start()
        loads.append(load)

    early[0].wait()
    for h in range(2):
        low[h] = rhs_v[:, h * part:(h + 1) * part].astype(BF16)
    early[1].wait()
    early[2].wait()
    early[3].wait()

    @pl.when(row > 0)
    def _():
        coef = dot_t(guess_v[...].astype(BF16), right_v[...].reshape(nb * width, m))
        for i in range(nb - 1):
            c_out[i] = fold(coef[:, i * width:(i + 1) * width])

    pl.semaphore_wait(barrier, nc * nz - 1 + row * (nc * nz))

    for i in range(nb - 1):
        for k, (dc, dz) in enumerate(around):
            start(row > i, remote(c_out.at[i], c_in.at[row, col, z], c_send.at[i, k], c_recv.at[row, col, z], there(i, dc, dz)))

    mine = pl.ds(pl.multiple_of(z * slots, slots), slots)

    def send_x(pred):
        for c in range(nc):
            start(
                pred & jnp.logical_not(diag & (col == c)),
                remote(low.at[c % 2], x.at[c % 2, mine], x_send.at[c], x_recv.at[z], (row, c, col)),
            )

    def own(q):
        return pltpu.make_async_copy(
            left_ref.at[0, lax.rem(row + 1 + q, nb), :, pl.ds(pl.multiple_of(half * part, part), part)],
            lf.at[q, half], own_sem.at[q],
        )

    send_x(row == 0)
    for q in range(nb - 1):
        block = lax.rem(row + 1 + q, nb)
        for c in range(nc):
            start(
                diag & (col != c),
                remote(
                    left_ref.at[0, block, :, pl.ds((c % 2) * part, part)], lf.at[q, c % 2],
                    l_send.at[q, c], l_recv.at[q], (row, c, z),
                ),
            )
    send_x(row > 0)

    @pl.when(diag)
    def _():
        for q in range(nb - 1):
            own(q).start()
        x[half, mine] = low[half]

    def wait_left(q):
        @pl.when(diag)
        def _():
            own(q).wait()

        @pl.when(jnp.logical_not(diag))
        def _():
            spot = lf.at[q, half]
            remote(spot, spot, l_send.at[0, 0], l_recv.at[q], sibling).wait_recv()

    def wait_x():
        for zz in range(nz):
            @pl.when(jnp.logical_not(diag & (z == zz)))
            def _():
                spot = x.at[half, pl.ds(zz * slots, slots)]
                remote(spot, spot, x_send.at[0], x_recv.at[zz], sibling).wait_recv()

    def send_new(t, i):
        for k, (dc, dz) in enumerate(around):
            start(
                row == t,
                remote(n_out.at[i], n_in.at[t, col, z], n_send.at[i, k], n_recv.at[t, col, z], there(i, dc, dz)),
            )

    strip = part // 4
    for t in range(nb - 1):
        later = nb - 1 - t

        @pl.when(row == t)
        def _():
            span = pl.ds(0, later)
            swap = remote(a_out.at[span], a_in.at[span], a_send, a_recv, sibling)
            loads[0].wait()

            def theirs(i, _):
                cut = pl.ds(pl.multiple_of(i * strip, strip), strip)
                for b in range(later):
                    a_out[b, cut] = dot_t(inv[1 - half, cut], right_v[t + 1 + b]).astype(BF16)
                return _

            lax.fori_loop(0, part // strip, theirs, 0)
            swap.start()
            loads[1].wait()

            def kept(i, _):
                cut = pl.ds(pl.multiple_of(i * strip, strip), strip)
                for b in range(later):
                    a_own[b, cut] = dot_t(inv[half, cut], right_v[t + 1 + b])
                return _

            lax.fori_loop(0, part // strip, kept, 0)
            swap.wait()
            for b in range(later):
                a_sum[b] = (a_own[b] + a_in[b].astype(F32)).astype(BF16)

    def paired(t):
        span = pl.ds(0, t * width)
        return remote(li_out.at[span], li_in.at[span], li_send, li_recv, (row, col, z + 1 - 2 * lax.rem(z, 2)))

    def columns(which, i=0, size=wide):
        return pl.ds(pl.multiple_of(which * wide + i * size, size), size)

    ours = lax.rem(z, 2)

    for t in range(1, nb):
        later = nb - 1 - t
        tall = t * width

        @pl.when(row == t)
        def _():
            swaps = []
            for q in range(later, nb - 1):
                wait_left(q)
                spot = lf.at[q, half]
                copy = remote(spot, spot, ls_send.at[q], ls_recv.at[q], sibling)
                copy.start()
                swaps.append(copy)
            if not later:
                loads[0].wait()

            def first(i, _):
                cut = pl.ds(pl.multiple_of(i * TILE, TILE), TILE)
                p_left[:tall, cut] = dot(lf[later:, half].reshape(tall, part), inv[half, :, cut])
                return _

            lax.fori_loop(0, m // TILE, first, 0)
            if not later:
                loads[1].wait()
            for copy in swaps:
                copy.wait_recv()

            def second(i, _):
                cut = columns(1 - ours, i, TILE)
                value = p_left[:tall, cut] + dot(lf[later:, 1 - half].reshape(tall, part), inv[1 - half, :, cut])
                li_out[:tall, pl.ds(pl.multiple_of(i * TILE, TILE), TILE)] = value.astype(BF16)
                return _

            def third(i, _):
                cut = columns(ours, i, TILE)
                p_left[:tall, cut] += dot(lf[later:, 1 - half].reshape(tall, part), inv[1 - half, :, cut])
                return _

            lax.fori_loop(0, wide // TILE, second, 0)
            paired(t).start()
            lax.fori_loop(0, wide // TILE, third, 0)
            for copy in swaps:
                copy.wait_send()

    swap = remote(x.at[half], x.at[half], sib_send, sib_recv, sibling)
    for t in range(nb):
        later = nb - 1 - t

        @pl.when(row == t)
        def _():
            if later:
                blocks = []
                for j in range(t + 1, nb):
                    parts = []
                    for zz in range(nz):
                        total = None
                        for c in range(nc):
                            spot = c_in.at[j, c, zz]
                            remote(spot, spot, c_send.at[0, 0], c_recv.at[j, c, zz], sibling).wait_recv()
                            term = c_in[j, c, zz]
                            total = term if total is None else total + term
                        parts.append(unfold(total))
                    whole = jnp.concatenate(parts, axis=0)
                    lane = lax.broadcasted_iota(jnp.int32, whole.shape, 1)
                    blocks.append(jnp.where(lane < ranks_ref[t, j], whole, jnp.zeros_like(whole)).astype(BF16))
                coefs = blocks[0] if later == 1 else jnp.concatenate(blocks, axis=1)
                for q in range(later):
                    wait_left(q)
            wait_x()
            if later:
                coupled = dot(coefs, lf[:later, half].reshape(later * width, part))
                rest = (x[half].astype(F32) - coupled).astype(BF16)
                x[half] = rest
            swap.start()
            if later:
                for i in range(t + 1, nb):
                    share = dot(rest, a_sum[i - t - 1])
                    if t:
                        p_new[i] = share
                        for j in range(t):
                            q_new[i, j] = dot(lf[later + j, half], a_sum[i - t - 1])
                    else:
                        n_out[i] = fold(share).astype(BF16)

    for i in range(1, nb):
        send_new(0, i)

    def first(i, _):
        cut = pl.ds(pl.multiple_of(i * TILE, TILE), TILE)
        p_rhs[:, cut] = dot(x[half], inv[half, :, cut])
        return _

    lax.fori_loop(0, m // TILE, first, 0)
    far = x.at[1 - half]
    remote(far, far, sib_send, sib_recv, sibling).wait_recv()

    span_m = m // CHUNKS
    others = [lax.rem(z + step, nz) for step in range(1, nz)]

    def pieces(ch):
        return [
            remote(
                s_out.at[ch, other], s_in.at[ch, z], rs_send.at[ch, i], rs_recv.at[ch, z], (row, col, other)
            )
            for i, other in enumerate(others)
        ]

    def across(i, other):
        return remote(k_out.at[other], k_in.at[z], k_send.at[i], k_recv.at[z], (row, col, other))

    for ch in range(CHUNKS):
        cut = slice(ch * span_m, (ch + 1) * span_m)
        now = p_rhs[:, cut] + dot(x[1 - half], inv[1 - half, :, cut])
        p_rhs[:, cut] = now
        for zz in range(nz):
            s_out[ch, zz] = now[zz * slots:(zz + 1) * slots].astype(BF16)
        for copy in pieces(ch):
            copy.start()
    swap.wait_send()

    for t in range(1, nb):
        later = nb - 1 - t
        tall = t * width

        @pl.when(row == t)
        def _():
            paired(t).wait_recv()
            li_sum[:tall] = (p_left[:tall, columns(ours)] + li_in[:tall].astype(F32)).astype(BF16)
            blocks = []
            for j in range(t):
                total = None
                for c in range(nc):
                    for zz in range(nz):
                        spot = n_in.at[j, c, zz]
                        remote(spot, spot, n_send.at[0, 0], n_recv.at[j, c, zz], sibling).wait_recv()
                        term = n_in[j, c, zz].astype(F32)
                        total = term if total is None else total + term
                whole = unfold(total)
                lane = lax.broadcasted_iota(jnp.int32, whole.shape, 1)
                blocks.append(jnp.where(lane < ranks_ref[t, j], whole, jnp.zeros_like(whole)).astype(BF16))
            for i in range(t + 1, nb):
                share = p_new[i]
                for j in range(t):
                    share = share - dot(blocks[j], q_new[i, j].astype(BF16))
                n_out[i] = fold(share).astype(BF16)
            coefs = blocks[0] if t == 1 else jnp.concatenate(blocks, axis=1)
            coef_v[:, :tall] = coefs

        for i in range(t + 1, nb):
            send_new(t, i)

        @pl.when(row == t)
        def _():
            value = dot(coef_v[:, :tall], li_sum[:tall])
            for zz in range(nz):
                k_out[zz] = value[zz * slots:(zz + 1) * slots].astype(BF16)
            for i, other in enumerate(others):
                across(i, other).start()
            k_all[...] = value

    for ch in range(CHUNKS):
        cut = slice(ch * span_m, (ch + 1) * span_m)
        total = p_rhs[mine, cut]
        for other in others:
            spot = s_in.at[ch, other]
            remote(spot, spot, rs_send.at[0, 0], rs_recv.at[ch, other], (row, col, other)).wait_recv()
            total = total + s_in[ch, other].astype(F32)
        out_ref[0, :, cut] = total

    @pl.when(row > 0)
    def _():
        def take(which, value):
            cut = columns(which)
            out_ref[0, :, cut] = out_ref[0, :, cut] - value

        take(ours, k_all[mine])
        for other in others:
            spot = k_in.at[other]
            remote(spot, spot, k_send.at[0], k_recv.at[other], (row, col, other)).wait_recv()
            take(lax.rem(other, 2), k_in[other].astype(F32))
        for i, other in enumerate(others):
            across(i, other).wait_send()

    for t in range(1, nb):
        @pl.when(row == t)
        def _():
            paired(t).wait_send()
    for ch in range(CHUNKS):
        for copy in pieces(ch):
            copy.wait_send()
    for pred, copy in sent:
        @pl.when(pred)
        def _():
            copy.wait_send()


def solution(mesh):
    nb, nc, nz = mesh.shape["row"], mesh.shape["col"], mesh.shape["rhs"]

    def body(right_side, guess, inverse, left_factor, right_factor, ranks):
        slots, m = right_side.shape[1:]
        width = left_factor.shape[2]
        rows = nz * slots
        part = inverse.shape[1] // 2
        pairs = nb - 1
        tall = pairs * width
        wide = m // 2
        dma = pltpu.SemaphoreType.DMA
        hbm = pl.BlockSpec(memory_space=pltpu.HBM)
        vmem = pl.BlockSpec(memory_space=pltpu.VMEM)
        arrays = [
            pltpu.with_memory_space_constraint(array, pltpu.HBM)
            for array in (right_side, guess, inverse, left_factor, right_factor, ranks)
        ]
        return pl.pallas_call(
            functools.partial(kernel, nb, nc, nz, width),
            out_shape=jax.ShapeDtypeStruct(right_side.shape, F32),
            in_specs=[
                hbm, hbm, hbm, hbm, hbm,
                hbm,
            ],
            out_specs=vmem,
            scratch_shapes=[
                pltpu.VMEM((2, part, m), BF16),
                pltpu.VMEM((slots, m), F32),
                pltpu.VMEM((slots, m), F32),
                pltpu.VMEM((nb, width, m), BF16),
                pltpu.VMEM((2, slots, part), BF16),
                pltpu.VMEM((2, rows, part), BF16),
                pltpu.VMEM((pairs, 2, width, part), BF16),
                pltpu.VMEM((rows, m), F32),
                pltpu.VMEM((tall, m), F32),
                pltpu.VMEM((pairs, part, width), BF16),
                pltpu.VMEM((pairs, part, width), BF16),
                pltpu.VMEM((pairs, part, width), F32),
                pltpu.VMEM((pairs, part, width), BF16),
                pltpu.VMEM((pairs, slots // 2, 2 * width), F32),
                pltpu.VMEM((nb, nc, nz, slots // 2, 2 * width), F32),
                pltpu.VMEM((nb, rows // 2, 2 * width), BF16),
                pltpu.VMEM((pairs, nc, nz, rows // 2, 2 * width), BF16),
                pltpu.VMEM((nb, rows, width), F32),
                pltpu.VMEM((nb, nb, width, width), F32),
                pltpu.VMEM((tall, wide), BF16),
                pltpu.VMEM((tall, wide), BF16),
                pltpu.VMEM((CHUNKS, nz, slots, m // CHUNKS), BF16),
                pltpu.VMEM((CHUNKS, nz, slots, m // CHUNKS), BF16),
                pltpu.VMEM((nz, slots, wide), BF16),
                pltpu.VMEM((nz, slots, wide), BF16),
                pltpu.VMEM((rows, wide), F32),
                pltpu.VMEM((rows, tall), BF16),
                pltpu.VMEM((tall, wide), BF16),
                pltpu.SMEM(ranks.shape, jnp.int32),
                dma((2,)), dma((4,)), dma((pairs,)),
                dma((nc,)), dma((nz,)),
                dma((pairs, nc)), dma((pairs,)),
                dma((pairs,)), dma((pairs,)),
                dma, dma,
                dma, dma,
                dma((pairs, nc * nz)), dma((nb, nc, nz)),
                dma((nb, nc * nz)), dma((pairs, nc, nz)),
                dma, dma,
                dma((CHUNKS, nz - 1)), dma((CHUNKS, nz)),
                dma((nz - 1,)), dma((nz,)),
            ],
            compiler_params=pltpu.CompilerParams(
                collective_id=0, has_side_effects=True, vmem_limit_bytes=40 * 1024 * 1024
            ),
        )(*arrays)

    in_specs = (
        P("row", "rhs", "col"),
        P("row", "rhs", "col"),
        P("row", "rhs", "col"),
        P("row", None, None, "col"),
        P("row", None, None, "col"),
        P(),
    )
    out_specs = P("row", "rhs", "col")
    return jax.shard_map(body, mesh=mesh, in_specs=in_specs, out_specs=out_specs, check_vma=False)
```

```python
import functools

import jax
import jax.numpy as jnp
from jax import lax
from jax.experimental import pallas as pl
from jax.experimental.pallas import tpu as pltpu
from jax.sharding import PartitionSpec as P

F32 = jnp.float32
BF16 = jnp.bfloat16
TILE = 512
CHUNKS = 2


def dot(a, b):
    return lax.dot_general(a, b, (((1,), (0,)), ((), ())), preferred_element_type=F32)


def dot_t(a, b):
    return lax.dot_general(a, b, (((1,), (1,)), ((), ())), preferred_element_type=F32)


def fold(value):
    half = value.shape[0] // 2
    return jnp.concatenate([value[:half], value[half:]], axis=1)


def unfold(value):
    half = value.shape[1] // 2
    return jnp.concatenate([value[:, :half], value[:, half:]], axis=0)


def kernel(
    nb, nc, nz, width,
    rhs_ref, guess_ref, inv_ref, left_ref, right_ref, ranks_hbm, out_ref,
    inv, rhs_v, guess_v, right_v, low, x, lf, p_rhs, p_left,
    a_out, a_in, a_own, a_sum, c_out, c_in, n_out, n_in, p_new, q_new,
    li_out, li_in, s_out, s_in, k_out, k_in, k_all, y_out, y_in, w_out, w_in, coef_v, li_sum, ranks_ref,
    inv_sem, in_sem, own_sem, x_send, x_recv, l_send, l_recv, ls_send, ls_recv, sib_send, sib_recv,
    a_send, a_recv, c_send, c_recv, n_send, n_recv, li_send, li_recv, rs_send, rs_recv, k_send, k_recv, y_send, y_recv,
):
    row, col, z = lax.axis_index("row"), lax.axis_index("col"), lax.axis_index("rhs")
    slots, part = low.shape[1:]
    m = inv.shape[2]
    rows = nz * slots
    wide = m // 2
    half = col % 2
    sibling = (row, col + 1 - 2 * half, z)
    diag = col == z
    sent = []

    def remote(src, dst, send, recv, where):
        return pltpu.make_async_remote_copy(
            src_ref=src, dst_ref=dst, send_sem=send, recv_sem=recv,
            device_id=where, device_id_type=pl.DeviceIdType.MESH,
        )

    def start(pred, copy):
        @pl.when(pred)
        def _():
            copy.start()
        sent.append((pred, copy))

    around = [(dc, dz) for dz in range(nz) for dc in range(nc)]

    def there(r, dc, dz):
        return (r, lax.rem(col + dc, nc), lax.rem(z + dz, nz))

    barrier = pltpu.get_barrier_semaphore()
    for dc, dz in around[1:]:
        pl.semaphore_signal(barrier, inc=1, device_id=there(row, dc, dz), device_id_type=pl.DeviceIdType.MESH)
    for r in range(1, nb):
        @pl.when(row < r)
        def _():
            for dc, dz in around:
                pl.semaphore_signal(barrier, inc=1, device_id=there(r, dc, dz), device_id_type=pl.DeviceIdType.MESH)
    early = [
        pltpu.make_async_copy(src, dst, in_sem.at[i])
        for i, (src, dst) in enumerate(
            ((rhs_ref.at[0], rhs_v), (guess_ref.at[0], guess_v), (right_ref.at[0], right_v), (ranks_hbm, ranks_ref))
        )
    ]
    for load in early:
        load.start()
    ahead = jnp.where(row < nb - 1, 1 - half, half)
    loads = []
    for order in range(2):
        h = ahead if order == 0 else 1 - ahead
        load = pltpu.make_async_copy(
            inv_ref.at[0, pl.ds(pl.multiple_of(h * part, part), part)], inv.at[h], inv_sem.at[order]
        )
        load.start()
        loads.append(load)

    early[0].wait()
    for h in range(2):
        low[h] = rhs_v[:, h * part:(h + 1) * part].astype(BF16)
    early[1].wait()
    early[2].wait()
    early[3].wait()

    @pl.when(row > 0)
    def _():
        coef = dot_t(guess_v[...].astype(BF16), right_v[...].reshape(nb * width, m))
        for i in range(nb - 1):
            c_out[i] = fold(coef[:, i * width:(i + 1) * width])

    pl.semaphore_wait(barrier, nc * nz - 1 + row * (nc * nz))

    def send_left(pred):
        for q in range(nb - 1):
            block = lax.rem(row + 1 + q, nb)
            for c in range(nc):
                start(
                    pred & diag & (col != c),
                    remote(
                        left_ref.at[0, block, :, pl.ds((c % 2) * part, part)], lf.at[q, c % 2],
                        l_send.at[q, c], l_recv.at[q], (row, c, z),
                    ),
                )

    send_left(row > 0)
    for i in range(nb - 1):
        for k, (dc, dz) in enumerate(around):
            start(row > i, remote(c_out.at[i], c_in.at[row, col, z], c_send.at[i, k], c_recv.at[row, col, z], there(i, dc, dz)))

    mine = pl.ds(pl.multiple_of(z * slots, slots), slots)

    def send_x(pred):
        for c in range(nc):
            start(
                pred & jnp.logical_not(diag & (col == c)),
                remote(low.at[c % 2], x.at[c % 2, mine], x_send.at[c], x_recv.at[z], (row, c, col)),
            )

    def own(q):
        return pltpu.make_async_copy(
            left_ref.at[0, lax.rem(row + 1 + q, nb), :, pl.ds(pl.multiple_of(half * part, part), part)],
            lf.at[q, half], own_sem.at[q],
        )

    send_x(row == 0)
    send_left(row == 0)
    send_x(row > 0)

    @pl.when(diag)
    def _():
        for q in range(nb - 1):
            own(q).start()
        x[half, mine] = low[half]

    def wait_left(q):
        @pl.when(diag)
        def _():
            own(q).wait()

        @pl.when(jnp.logical_not(diag))
        def _():
            spot = lf.at[q, half]
            remote(spot, spot, l_send.at[0, 0], l_recv.at[q], sibling).wait_recv()

    def wait_x():
        for zz in range(nz):
            @pl.when(jnp.logical_not(diag & (z == zz)))
            def _():
                spot = x.at[half, pl.ds(zz * slots, slots)]
                remote(spot, spot, x_send.at[0], x_recv.at[zz], sibling).wait_recv()

    def send_new(t, i):
        for k, (dc, dz) in enumerate(around):
            start(
                row == t,
                remote(n_out.at[i], n_in.at[t, col, z], n_send.at[i, k], n_recv.at[t, col, z], there(i, dc, dz)),
            )

    strip = part // 4
    for t in range(nb - 1):
        later = nb - 1 - t

        @pl.when(row == t)
        def _():
            span = pl.ds(0, later)
            swap = remote(a_out.at[span], a_in.at[span], a_send, a_recv, sibling)
            loads[0].wait()

            def theirs(i, _):
                cut = pl.ds(pl.multiple_of(i * strip, strip), strip)
                for b in range(later):
                    a_out[b, cut] = dot_t(inv[1 - half, cut], right_v[t + 1 + b]).astype(BF16)
                return _

            lax.fori_loop(0, part // strip, theirs, 0)
            swap.start()
            loads[1].wait()

            def kept(i, _):
                cut = pl.ds(pl.multiple_of(i * strip, strip), strip)
                for b in range(later):
                    a_own[b, cut] = dot_t(inv[half, cut], right_v[t + 1 + b])
                return _

            lax.fori_loop(0, part // strip, kept, 0)
            swap.wait()
            for b in range(later):
                a_sum[b] = (a_own[b] + a_in[b].astype(F32)).astype(BF16)

    def paired(t):
        span = pl.ds(0, t * width)
        return remote(li_out.at[span], li_in.at[span], li_send, li_recv, (row, col, z + 1 - 2 * lax.rem(z, 2)))

    def columns(which, i=0, size=wide):
        return pl.ds(pl.multiple_of(which * wide + i * size, size), size)

    ours = lax.rem(z, 2)

    for t in range(1, nb):
        later = nb - 1 - t
        tall = t * width

        @pl.when(row == t)
        def _():
            swaps = []
            for q in range(later, nb - 1):
                wait_left(q)
                spot = lf.at[q, half]
                copy = remote(spot, spot, ls_send.at[q], ls_recv.at[q], sibling)
                copy.start()
                swaps.append(copy)
            if not later:
                loads[0].wait()

            def first(i, _):
                cut = pl.ds(pl.multiple_of(i * TILE, TILE), TILE)
                p_left[:tall, cut] = dot(lf[later:, half].reshape(tall, part), inv[half, :, cut])
                return _

            lax.fori_loop(0, m // TILE, first, 0)
            if not later:
                loads[1].wait()
            for copy in swaps:
                copy.wait_recv()

            def second(i, _):
                cut = columns(1 - ours, i, TILE)
                value = p_left[:tall, cut] + dot(lf[later:, 1 - half].reshape(tall, part), inv[1 - half, :, cut])
                li_out[:tall, pl.ds(pl.multiple_of(i * TILE, TILE), TILE)] = value.astype(BF16)
                return _

            def third(i, _):
                cut = columns(ours, i, TILE)
                p_left[:tall, cut] += dot(lf[later:, 1 - half].reshape(tall, part), inv[1 - half, :, cut])
                return _

            lax.fori_loop(0, wide // TILE, second, 0)
            paired(t).start()
            lax.fori_loop(0, wide // TILE, third, 0)
            for copy in swaps:
                copy.wait_send()

    swap = remote(x.at[half], x.at[half], sib_send, sib_recv, sibling)
    for t in range(nb):
        later = nb - 1 - t

        @pl.when(row == t)
        def _():
            if later:
                blocks = []
                for j in range(t + 1, nb):
                    parts = []
                    for zz in range(nz):
                        total = None
                        for c in range(nc):
                            spot = c_in.at[j, c, zz]
                            remote(spot, spot, c_send.at[0, 0], c_recv.at[j, c, zz], sibling).wait_recv()
                            term = c_in[j, c, zz]
                            total = term if total is None else total + term
                        parts.append(unfold(total))
                    whole = jnp.concatenate(parts, axis=0)
                    lane = lax.broadcasted_iota(jnp.int32, whole.shape, 1)
                    blocks.append(jnp.where(lane < ranks_ref[t, j], whole, jnp.zeros_like(whole)).astype(BF16))
                coefs = blocks[0] if later == 1 else jnp.concatenate(blocks, axis=1)
                for q in range(later):
                    wait_left(q)
            wait_x()
            if later:
                coupled = dot(coefs, lf[:later, half].reshape(later * width, part))
                rest = (x[half].astype(F32) - coupled).astype(BF16)
                x[half] = rest
            swap.start()
            if later:
                for i in range(t + 1, nb):
                    share = dot(rest, a_sum[i - t - 1])
                    if t:
                        p_new[i] = share
                        for j in range(t):
                            q_new[i, j] = dot(lf[later + j, half], a_sum[i - t - 1])
                    else:
                        n_out[i] = fold(share).astype(BF16)

    for i in range(1, nb):
        send_new(0, i)

    def first(i, _):
        cut = pl.ds(pl.multiple_of(i * TILE, TILE), TILE)
        p_rhs[:, cut] = dot(x[half], inv[half, :, cut])
        return _

    lax.fori_loop(0, m // TILE, first, 0)
    far = x.at[1 - half]
    remote(far, far, sib_send, sib_recv, sibling).wait_recv()

    span_m = m // CHUNKS
    others = [lax.rem(z + step, nz) for step in range(1, nz)]

    def pieces(ch):
        return [
            remote(
                s_out.at[ch, other], s_in.at[ch, z], rs_send.at[ch, i], rs_recv.at[ch, z], (row, col, other)
            )
            for i, other in enumerate(others)
        ]

    def across(i, other):
        return remote(k_out.at[other], k_in.at[z], k_send.at[i], k_recv.at[z], (row, col, other))

    partner = z + 1 - 2 * ours
    beyond = [lax.rem(z - ours + 2 * step + e, nz) for step in range(1, nz // 2) for e in range(2)]
    outer = remote(y_out, y_in, y_send.at[0], y_recv.at[0], (row, col, partner))
    inner = remote(w_out, w_in, y_send.at[1], y_recv.at[1], (row, col, partner))

    def block(which):
        return pl.ds(pl.multiple_of(which * slots, slots), slots)

    def second(which):
        def tile(i, _):
            cut = columns(which, i, TILE)
            p_rhs[:, cut] += dot(x[1 - half], inv[1 - half, :, cut])
            return _

        lax.fori_loop(0, wide // TILE, tile, 0)

    @pl.when(row == 0)
    def _():
        for ch in range(CHUNKS):
            cut = slice(ch * span_m, (ch + 1) * span_m)
            now = p_rhs[:, cut] + dot(x[1 - half], inv[1 - half, :, cut])
            p_rhs[:, cut] = now
            for zz in range(nz):
                s_out[ch, zz] = now[zz * slots:(zz + 1) * slots].astype(BF16)
            for copy in pieces(ch):
                copy.start()

    @pl.when(row > 0)
    def _():
        second(1 - ours)
        for k, other in enumerate(beyond):
            y_out[k] = p_rhs[block(other), columns(1 - ours)].astype(BF16)
        outer.start()
        second(ours)
        w_out[...] = p_rhs[block(partner)].astype(BF16)
        inner.start()

    swap.wait_send()

    for t in range(1, nb):
        later = nb - 1 - t
        tall = t * width

        @pl.when(row == t)
        def _():
            paired(t).wait_recv()
            li_sum[:tall] = (p_left[:tall, columns(ours)] + li_in[:tall].astype(F32)).astype(BF16)
            blocks = []
            for j in range(t):
                total = None
                for c in range(nc):
                    for zz in range(nz):
                        spot = n_in.at[j, c, zz]
                        remote(spot, spot, n_send.at[0, 0], n_recv.at[j, c, zz], sibling).wait_recv()
                        term = n_in[j, c, zz].astype(F32)
                        total = term if total is None else total + term
                whole = unfold(total)
                lane = lax.broadcasted_iota(jnp.int32, whole.shape, 1)
                blocks.append(jnp.where(lane < ranks_ref[t, j], whole, jnp.zeros_like(whole)).astype(BF16))
            for i in range(t + 1, nb):
                share = p_new[i]
                for j in range(t):
                    share = share - dot(blocks[j], q_new[i, j].astype(BF16))
                n_out[i] = fold(share).astype(BF16)
            coefs = blocks[0] if t == 1 else jnp.concatenate(blocks, axis=1)
            coef_v[:, :tall] = coefs

        for i in range(t + 1, nb):
            send_new(t, i)

        @pl.when(row == t)
        def _():
            k_all[...] = dot(coef_v[:, :tall], li_sum[:tall])
            outer.wait_recv()
            for k, other in enumerate(beyond):
                value = p_rhs[block(other), columns(ours)] + y_in[k].astype(F32) - k_all[block(other)]
                k_out[other] = value.astype(BF16)
                across(k, other).start()
            k_out[partner] = (-k_all[block(partner)]).astype(BF16)
            across(nz - 2, partner).start()

    @pl.when(row == 0)
    def _():
        for ch in range(CHUNKS):
            cut = slice(ch * span_m, (ch + 1) * span_m)
            total = p_rhs[mine, cut]
            for other in others:
                spot = s_in.at[ch, other]
                remote(spot, spot, rs_send.at[0, 0], rs_recv.at[ch, other], (row, col, other)).wait_recv()
                total = total + s_in[ch, other].astype(F32)
            out_ref[0, :, cut] = total
        for ch in range(CHUNKS):
            for copy in pieces(ch):
                copy.wait_send()

    @pl.when(row > 0)
    def _():
        inner.wait_recv()
        p_rhs[mine, columns(ours)] -= k_all[mine]
        total = p_rhs[mine] + w_in[...].astype(F32)
        out_ref[0] = total
        for other in [partner] + beyond:
            spot = k_in.at[other]
            remote(spot, spot, k_send.at[0], k_recv.at[other], (row, col, other)).wait_recv()
            cut = columns(lax.rem(other, 2))
            out_ref[0, :, cut] = out_ref[0, :, cut] + k_in[other].astype(F32)
        for k, other in enumerate(beyond + [partner]):
            across(k, other).wait_send()
        outer.wait_send()
        inner.wait_send()

    for t in range(1, nb):
        @pl.when(row == t)
        def _():
            paired(t).wait_send()
    for pred, copy in sent:
        @pl.when(pred)
        def _():
            copy.wait_send()


def solution(mesh):
    nb, nc, nz = mesh.shape["row"], mesh.shape["col"], mesh.shape["rhs"]

    def body(right_side, guess, inverse, left_factor, right_factor, ranks):
        slots, m = right_side.shape[1:]
        width = left_factor.shape[2]
        rows = nz * slots
        part = inverse.shape[1] // 2
        pairs = nb - 1
        tall = pairs * width
        wide = m // 2
        dma = pltpu.SemaphoreType.DMA
        hbm = pl.BlockSpec(memory_space=pltpu.HBM)
        vmem = pl.BlockSpec(memory_space=pltpu.VMEM)
        arrays = [
            pltpu.with_memory_space_constraint(array, pltpu.HBM)
            for array in (right_side, guess, inverse, left_factor, right_factor, ranks)
        ]
        return pl.pallas_call(
            functools.partial(kernel, nb, nc, nz, width),
            out_shape=jax.ShapeDtypeStruct(right_side.shape, F32),
            in_specs=[
                hbm, hbm, hbm, hbm, hbm,
                hbm,
            ],
            out_specs=vmem,
            scratch_shapes=[
                pltpu.VMEM((2, part, m), BF16),
                pltpu.VMEM((slots, m), F32),
                pltpu.VMEM((slots, m), F32),
                pltpu.VMEM((nb, width, m), BF16),
                pltpu.VMEM((2, slots, part), BF16),
                pltpu.VMEM((2, rows, part), BF16),
                pltpu.VMEM((pairs, 2, width, part), BF16),
                pltpu.VMEM((rows, m), F32),
                pltpu.VMEM((tall, m), F32),
                pltpu.VMEM((pairs, part, width), BF16),
                pltpu.VMEM((pairs, part, width), BF16),
                pltpu.VMEM((pairs, part, width), F32),
                pltpu.VMEM((pairs, part, width), BF16),
                pltpu.VMEM((pairs, slots // 2, 2 * width), F32),
                pltpu.VMEM((nb, nc, nz, slots // 2, 2 * width), F32),
                pltpu.VMEM((nb, rows // 2, 2 * width), BF16),
                pltpu.VMEM((pairs, nc, nz, rows // 2, 2 * width), BF16),
                pltpu.VMEM((nb, rows, width), F32),
                pltpu.VMEM((nb, nb, width, width), F32),
                pltpu.VMEM((tall, wide), BF16),
                pltpu.VMEM((tall, wide), BF16),
                pltpu.VMEM((CHUNKS, nz, slots, m // CHUNKS), BF16),
                pltpu.VMEM((CHUNKS, nz, slots, m // CHUNKS), BF16),
                pltpu.VMEM((nz, slots, wide), BF16),
                pltpu.VMEM((nz, slots, wide), BF16),
                pltpu.VMEM((rows, wide), F32),
                pltpu.VMEM((nz - 2, slots, wide), BF16),
                pltpu.VMEM((nz - 2, slots, wide), BF16),
                pltpu.VMEM((slots, m), BF16),
                pltpu.VMEM((slots, m), BF16),
                pltpu.VMEM((rows, tall), BF16),
                pltpu.VMEM((tall, wide), BF16),
                pltpu.SMEM(ranks.shape, jnp.int32),
                dma((2,)), dma((4,)), dma((pairs,)),
                dma((nc,)), dma((nz,)),
                dma((pairs, nc)), dma((pairs,)),
                dma((pairs,)), dma((pairs,)),
                dma, dma,
                dma, dma,
                dma((pairs, nc * nz)), dma((nb, nc, nz)),
                dma((nb, nc * nz)), dma((pairs, nc, nz)),
                dma, dma,
                dma((CHUNKS, nz - 1)), dma((CHUNKS, nz)),
                dma((nz - 1,)), dma((nz,)),
                dma((2,)), dma((2,)),
            ],
            compiler_params=pltpu.CompilerParams(
                collective_id=0, has_side_effects=True, vmem_limit_bytes=40 * 1024 * 1024
            ),
        )(*arrays)

    in_specs = (
        P("row", "rhs", "col"),
        P("row", "rhs", "col"),
        P("row", "rhs", "col"),
        P("row", None, None, "col"),
        P("row", None, None, "col"),
        P(),
    )
    out_specs = P("row", "rhs", "col")
    return jax.shard_map(body, mesh=mesh, in_specs=in_specs, out_specs=out_specs, check_vma=False)
```

```python
import functools

import jax
import jax.numpy as jnp
from jax import lax
from jax.experimental import pallas as pl
from jax.experimental.pallas import tpu as pltpu
from jax.sharding import PartitionSpec as P

F32 = jnp.float32
BF16 = jnp.bfloat16
TILE = 1024
CHUNKS = 1


def dot(a, b):
    return lax.dot_general(a, b, (((1,), (0,)), ((), ())), preferred_element_type=F32)


def dot_t(a, b):
    return lax.dot_general(a, b, (((1,), (1,)), ((), ())), preferred_element_type=F32)


def fold(value):
    half = value.shape[0] // 2
    return jnp.concatenate([value[:half], value[half:]], axis=1)


def unfold(value):
    half = value.shape[1] // 2
    return jnp.concatenate([value[:, :half], value[:, half:]], axis=0)


def kernel(
    nb, nc, nz, width,
    rhs_ref, guess_ref, inv_ref, left_ref, right_ref, ranks_hbm, out_ref,
    inv, rhs_v, guess_v, right_v, low, x, lf, lv, p_rhs, p_left,
    a_out, a_in, a_own, a_sum, c_out, c_in, n_out, n_in, ns_out, ns_in, p_new, q_new,
    li_out, li_in, s_out, s_in, k_out, k_in, k_all, y_out, y_in, w_out, w_in, coef_v, li_sum, ranks_ref,
    inv_sem, in_sem, own_sem, lv_sem, x_send, x_recv, l_send, l_recv, ls_send, ls_recv, sib_send, sib_recv,
    a_send, a_recv, c_send, c_recv, n_send, n_recv, ns_send, ns_recv, li_send, li_recv, rs_send, rs_recv, k_send, k_recv, y_send, y_recv,
):
    row, col, z = lax.axis_index("row"), lax.axis_index("col"), lax.axis_index("rhs")
    slots, part = low.shape[1:]
    m = inv.shape[2]
    rows = nz * slots
    wide = m // 2
    half = col % 2
    sibling = (row, col + 1 - 2 * half, z)
    diag = col == z
    sent = []

    def remote(src, dst, send, recv, where):
        return pltpu.make_async_remote_copy(
            src_ref=src, dst_ref=dst, send_sem=send, recv_sem=recv,
            device_id=where, device_id_type=pl.DeviceIdType.MESH,
        )

    def start(pred, copies):
        @pl.when(pred)
        def _():
            for copy in copies:
                copy.start()
        sent.append((pred, copies))

    def drain():
        for pred, copies in sent:
            @pl.when(pred)
            def _():
                for copy in copies:
                    copy.wait_send()
        sent.clear()

    around = [(dc, dz) for dz in range(nz) for dc in range(nc)]

    def there(r, dc, dz):
        return (r, lax.rem(col + dc, nc), lax.rem(z + dz, nz))

    barrier = pltpu.get_barrier_semaphore()
    for dc, dz in around[1:]:
        pl.semaphore_signal(barrier, inc=1, device_id=there(row, dc, dz), device_id_type=pl.DeviceIdType.MESH)
    for r in range(1, nb):
        @pl.when(row < r)
        def _():
            for dc, dz in around:
                pl.semaphore_signal(barrier, inc=1, device_id=there(r, dc, dz), device_id_type=pl.DeviceIdType.MESH)
    early = [
        pltpu.make_async_copy(src, dst, in_sem.at[i])
        for i, (src, dst) in enumerate(
            ((rhs_ref.at[0], rhs_v), (guess_ref.at[0], guess_v), (right_ref.at[0], right_v), (ranks_hbm, ranks_ref))
        )
    ]
    for load in early:
        load.start()
    shared = [
        pltpu.make_async_copy(
            left_ref.at[0, lax.rem(row + 1 + q, nb), :, pl.ds(h * part, part)], lv.at[q, h], lv_sem.at[q, h]
        )
        for q in range(nb - 1) for h in range(2)
    ]

    @pl.when(diag)
    def _():
        for load in shared:
            load.start()

    ahead = jnp.where(row < nb - 1, 1 - half, half)
    loads = []
    for order in range(2):
        h = ahead if order == 0 else 1 - ahead
        load = pltpu.make_async_copy(
            inv_ref.at[0, pl.ds(pl.multiple_of(h * part, part), part)], inv.at[h], inv_sem.at[order]
        )
        load.start()
        loads.append(load)

    early[0].wait()
    for h in range(2):
        low[h] = rhs_v[:, h * part:(h + 1) * part].astype(BF16)
    @pl.when(row > 0)
    def _():
        early[1].wait()
        early[2].wait()
        coef = dot_t(guess_v[...].astype(BF16), right_v[...].reshape(nb * width, m))
        for i in range(nb - 1):
            c_out[i] = fold(coef[:, i * width:(i + 1) * width])

    pl.semaphore_wait(barrier, nc * nz - 1 + row * (nc * nz))

    def send_left(pred):
        copies = []
        for q in range(nb - 1):
            for k in range(1, nc):
                c = lax.rem(col + k, nc)
                h = lax.rem(c, 2)
                copies.append(
                    remote(lv.at[q, h], lf.at[q, h], l_send.at[q, k], l_recv.at[q], (row, c, z))
                )

        @pl.when(pred & diag)
        def _():
            for load in shared:
                load.wait()

        start(pred & diag, copies)

    send_left(row > 0)
    for i in range(nb - 1):
        start(row > i, [
            remote(c_out.at[i], c_in.at[row, col, z], c_send.at[i, k], c_recv.at[row, col, z], there(i, dc, dz))
            for k, (dc, dz) in enumerate(around)
        ])

    mine = pl.ds(pl.multiple_of(z * slots, slots), slots)

    def send_x(pred):
        copies = []
        for k in range(nc):
            c = lax.rem(col + k, nc)
            h = lax.rem(c, 2)
            copies.append(remote(low.at[h], x.at[h, mine], x_send.at[k], x_recv.at[z], (row, c, col)))
        start(pred, copies[1:])
        start(pred & jnp.logical_not(diag), copies[:1])

    def own(q):
        return pltpu.make_async_copy(
            left_ref.at[0, lax.rem(row + 1 + q, nb), :, pl.ds(pl.multiple_of(half * part, part), part)],
            lf.at[q, half], own_sem.at[q],
        )

    send_x(row == 0)
    send_left(row == 0)
    send_x(row > 0)

    @pl.when(row == 0)
    def _():
        early[1].wait()
        early[2].wait()

    early[3].wait()

    @pl.when(diag)
    def _():
        for q in range(nb - 1):
            own(q).start()
        x[half, mine] = low[half]

    def wait_left(q):
        @pl.when(diag)
        def _():
            own(q).wait()

        @pl.when(jnp.logical_not(diag))
        def _():
            spot = lf.at[q, half]
            remote(spot, spot, l_send.at[0, 0], l_recv.at[q], sibling).wait_recv()

    def wait_x():
        for zz in range(nz):
            @pl.when(jnp.logical_not(diag & (z == zz)))
            def _():
                spot = x.at[half, pl.ds(zz * slots, slots)]
                remote(spot, spot, x_send.at[0], x_recv.at[zz], sibling).wait_recv()

    def send_new(t, i):
        start(row == t, [
            remote(n_out.at[i], n_in.at[t, col // 2, z], n_send.at[i, k], n_recv.at[t, col // 2, z], there(i, dc, dz))
            for k, (dc, dz) in enumerate(around) if dc % 2 == 0
        ])

    strip = part // 4
    for t in range(nb - 1):
        later = nb - 1 - t

        @pl.when(row == t)
        def _():
            span = pl.ds(0, later)
            swap = remote(a_out.at[span], a_in.at[span], a_send, a_recv, sibling)
            loads[0].wait()

            def theirs(i, _):
                cut = pl.ds(pl.multiple_of(i * strip, strip), strip)
                for b in range(later):
                    a_out[b, cut] = dot_t(inv[1 - half, cut], right_v[t + 1 + b]).astype(BF16)
                return _

            lax.fori_loop(0, part // strip, theirs, 0)
            swap.start()
            loads[1].wait()

            def kept(i, _):
                cut = pl.ds(pl.multiple_of(i * strip, strip), strip)
                for b in range(later):
                    a_own[b, cut] = dot_t(inv[half, cut], right_v[t + 1 + b])
                return _

            lax.fori_loop(0, part // strip, kept, 0)
            swap.wait()
            for b in range(later):
                a_sum[b] = (a_own[b] + a_in[b].astype(F32)).astype(BF16)

    def paired(t):
        span = pl.ds(0, t * width)
        return remote(li_out.at[span], li_in.at[span], li_send, li_recv, (row, col, z + 1 - 2 * lax.rem(z, 2)))

    def columns(which, i=0, size=wide):
        return pl.ds(pl.multiple_of(which * wide + i * size, size), size)

    ours = lax.rem(z, 2)

    for t in range(1, nb):
        later = nb - 1 - t
        tall = t * width

        @pl.when(row == t)
        def _():
            swaps = []
            for q in range(later, nb - 1):
                wait_left(q)
                spot = lf.at[q, half]
                copy = remote(spot, spot, ls_send.at[q], ls_recv.at[q], sibling)
                copy.start()
                swaps.append(copy)
            if not later:
                loads[0].wait()

            def first(i, _):
                cut = pl.ds(pl.multiple_of(i * TILE, TILE), TILE)
                p_left[:tall, cut] = dot(lf[later:, half].reshape(tall, part), inv[half, :, cut])
                return _

            lax.fori_loop(0, m // TILE, first, 0)
            if not later:
                loads[1].wait()
            for copy in swaps:
                copy.wait_recv()

            def second(i, _):
                cut = columns(1 - ours, i, TILE)
                value = p_left[:tall, cut] + dot(lf[later:, 1 - half].reshape(tall, part), inv[1 - half, :, cut])
                li_out[:tall, pl.ds(pl.multiple_of(i * TILE, TILE), TILE)] = value.astype(BF16)
                return _

            def third(i, _):
                cut = columns(ours, i, TILE)
                p_left[:tall, cut] += dot(lf[later:, 1 - half].reshape(tall, part), inv[1 - half, :, cut])
                return _

            lax.fori_loop(0, wide // TILE, second, 0)
            paired(t).start()
            lax.fori_loop(0, wide // TILE, third, 0)
            for copy in swaps:
                copy.wait_send()

    swap = remote(x.at[half], x.at[half], sib_send, sib_recv, sibling)
    for t in range(nb):
        later = nb - 1 - t

        @pl.when(row == t)
        def _():
            if later:
                blocks = []
                for j in range(t + 1, nb):
                    parts = []
                    for zz in range(nz):
                        total = None
                        for c in range(nc):
                            spot = c_in.at[j, c, zz]
                            remote(spot, spot, c_send.at[0, 0], c_recv.at[j, c, zz], sibling).wait_recv()
                            term = c_in[j, c, zz]
                            total = term if total is None else total + term
                        parts.append(unfold(total))
                    whole = jnp.concatenate(parts, axis=0)
                    lane = lax.broadcasted_iota(jnp.int32, whole.shape, 1)
                    blocks.append(jnp.where(lane < ranks_ref[t, j], whole, jnp.zeros_like(whole)).astype(BF16))
                coefs = blocks[0] if later == 1 else jnp.concatenate(blocks, axis=1)
                for q in range(later):
                    wait_left(q)
            wait_x()
            if later:
                coupled = dot(coefs, lf[:later, half].reshape(later * width, part))
                rest = (x[half].astype(F32) - coupled).astype(BF16)
                x[half] = rest
            swap.start()
            if later:
                for i in range(t + 1, nb):
                    share = dot(rest, a_sum[i - t - 1])
                    if t:
                        p_new[i] = share
                        for j in range(t):
                            q_new[i, j] = dot(lf[later + j, half], a_sum[i - t - 1])
                    else:
                        n_out[i] = fold(share).astype(BF16)

    for i in range(1, nb):
        send_new(0, i)

    @pl.when(row > 0)
    def _():
        def first(i, _):
            cut = pl.ds(pl.multiple_of(i * TILE, TILE), TILE)
            p_rhs[:, cut] = dot(x[half], inv[half, :, cut])
            return _

        lax.fori_loop(0, m // TILE, first, 0)

    far = x.at[1 - half]
    remote(far, far, sib_send, sib_recv, sibling).wait_recv()

    span_m = m // CHUNKS
    partner = z + 1 - 2 * ours
    beyond = [lax.rem(z - ours + 2 * step + e, nz) for step in range(1, nz // 2) for e in range(2)]
    others = beyond + [partner]

    def pieces(ch):
        return [
            remote(
                s_out.at[ch, other], s_in.at[ch, z], rs_send.at[ch, i], rs_recv.at[ch, z], (row, col, other)
            )
            for i, other in enumerate(others)
        ]

    def across(i, other):
        return remote(k_out.at[other], k_in.at[z], k_send.at[i], k_recv.at[z], (row, col, other))

    partner = z + 1 - 2 * ours
    beyond = [lax.rem(z - ours + 2 * step + e, nz) for step in range(1, nz // 2) for e in range(2)]
    outer = remote(y_out, y_in, y_send.at[0], y_recv.at[0], (row, col, partner))
    inner = remote(w_out, w_in, y_send.at[1], y_recv.at[1], (row, col, partner))

    def block(which):
        return pl.ds(pl.multiple_of(which * slots, slots), slots)

    def second(which):
        def tile(i, _):
            cut = columns(which, i, TILE)
            p_rhs[:, cut] += dot(x[1 - half], inv[1 - half, :, cut])
            return _

        lax.fori_loop(0, wide // TILE, tile, 0)

    @pl.when(row == 0)
    def _():
        for ch in range(CHUNKS):
            def tile(i, _):
                at = pl.ds(pl.multiple_of(i * TILE, TILE), TILE)
                cut = pl.ds(pl.multiple_of(ch * span_m + i * TILE, TILE), TILE)
                now = dot(x[half], inv[half, :, cut]) + dot(x[1 - half], inv[1 - half, :, cut])
                p_rhs[:, cut] = now
                for zz in range(nz):
                    s_out[ch, zz, :, at] = now[zz * slots:(zz + 1) * slots].astype(BF16)
                return _

            lax.fori_loop(0, span_m // TILE, tile, 0)
            for copy in pieces(ch):
                copy.start()

    @pl.when(row > 0)
    def _():
        second(1 - ours)
        for k, other in enumerate(beyond):
            y_out[k] = p_rhs[block(other), columns(1 - ours)].astype(BF16)
        outer.start()
        second(ours)
        w_out[...] = p_rhs[block(partner)].astype(BF16)
        inner.start()

    swap.wait_send()
    drain()

    for t in range(1, nb):
        later = nb - 1 - t
        tall = t * width

        @pl.when(row == t)
        def _():
            paired(t).wait_recv()
            li_sum[:tall] = (p_left[:tall, columns(ours)] + li_in[:tall].astype(F32)).astype(BF16)
            blocks = []
            for j in range(t):
                total = None
                for c in range(nc // 2):
                    for zz in range(nz):
                        spot = n_in.at[j, c, zz]
                        remote(spot, spot, n_send.at[0, 0], n_recv.at[j, c, zz], sibling).wait_recv()
                        term = n_in[j, c, zz].astype(F32)
                        total = term if total is None else total + term
                ns_out[j] = total
                other_half = remote(ns_out.at[j], ns_in.at[j], ns_send.at[j], ns_recv.at[j], sibling)
                other_half.start()
                other_half.wait()
                total = total + ns_in[j]
                whole = unfold(total)
                lane = lax.broadcasted_iota(jnp.int32, whole.shape, 1)
                blocks.append(jnp.where(lane < ranks_ref[t, j], whole, jnp.zeros_like(whole)).astype(BF16))
            for i in range(t + 1, nb):
                share = p_new[i]
                for j in range(t):
                    share = share - dot(blocks[j], q_new[i, j].astype(BF16))
                n_out[i] = fold(share).astype(BF16)
            coefs = blocks[0] if t == 1 else jnp.concatenate(blocks, axis=1)
            coef_v[:, :tall] = coefs

        for i in range(t + 1, nb):
            send_new(t, i)

        @pl.when(row == t)
        def _():
            k_all[...] = dot(coef_v[:, :tall], li_sum[:tall])
            outer.wait_recv()
            for k, other in enumerate(beyond):
                value = p_rhs[block(other), columns(ours)] + y_in[k].astype(F32) - k_all[block(other)]
                k_out[other] = value.astype(BF16)
                across(k, other).start()
            k_out[partner] = (-k_all[block(partner)]).astype(BF16)
            across(nz - 2, partner).start()

    @pl.when(row == 0)
    def _():
        for ch in range(CHUNKS):
            cut = slice(ch * span_m, (ch + 1) * span_m)
            total = p_rhs[mine, cut]
            for other in others:
                spot = s_in.at[ch, other]
                remote(spot, spot, rs_send.at[0, 0], rs_recv.at[ch, other], (row, col, other)).wait_recv()
                total = total + s_in[ch, other].astype(F32)
            out_ref[0, :, cut] = total
        for ch in range(CHUNKS):
            for copy in pieces(ch):
                copy.wait_send()

    @pl.when(row > 0)
    def _():
        inner.wait_recv()
        p_rhs[mine, columns(ours)] -= k_all[mine]
        total = p_rhs[mine] + w_in[...].astype(F32)
        out_ref[0] = total
        for other in [partner] + beyond:
            spot = k_in.at[other]
            remote(spot, spot, k_send.at[0], k_recv.at[other], (row, col, other)).wait_recv()
            cut = columns(lax.rem(other, 2))
            out_ref[0, :, cut] = out_ref[0, :, cut] + k_in[other].astype(F32)
        for k, other in enumerate(beyond + [partner]):
            across(k, other).wait_send()
        outer.wait_send()
        inner.wait_send()

    for t in range(1, nb):
        @pl.when(row == t)
        def _():
            paired(t).wait_send()
    drain()


def solution(mesh):
    nb, nc, nz = mesh.shape["row"], mesh.shape["col"], mesh.shape["rhs"]

    def body(right_side, guess, inverse, left_factor, right_factor, ranks):
        slots, m = right_side.shape[1:]
        width = left_factor.shape[2]
        rows = nz * slots
        part = inverse.shape[1] // 2
        pairs = nb - 1
        tall = pairs * width
        wide = m // 2
        dma = pltpu.SemaphoreType.DMA
        hbm = pl.BlockSpec(memory_space=pltpu.HBM)
        vmem = pl.BlockSpec(memory_space=pltpu.VMEM)
        arrays = [
            pltpu.with_memory_space_constraint(array, pltpu.HBM)
            for array in (right_side, guess, inverse, left_factor, right_factor, ranks)
        ]
        return pl.pallas_call(
            functools.partial(kernel, nb, nc, nz, width),
            out_shape=jax.ShapeDtypeStruct(right_side.shape, F32),
            in_specs=[
                hbm, hbm, hbm, hbm, hbm,
                hbm,
            ],
            out_specs=vmem,
            scratch_shapes=[
                pltpu.VMEM((2, part, m), BF16),
                pltpu.VMEM((slots, m), F32),
                pltpu.VMEM((slots, m), F32),
                pltpu.VMEM((nb, width, m), BF16),
                pltpu.VMEM((2, slots, part), BF16),
                pltpu.VMEM((2, rows, part), BF16),
                pltpu.VMEM((pairs, 2, width, part), BF16),
                pltpu.VMEM((pairs, 2, width, part), BF16),
                pltpu.VMEM((rows, m), F32),
                pltpu.VMEM((tall, m), F32),
                pltpu.VMEM((pairs, part, width), BF16),
                pltpu.VMEM((pairs, part, width), BF16),
                pltpu.VMEM((pairs, part, width), F32),
                pltpu.VMEM((pairs, part, width), BF16),
                pltpu.VMEM((pairs, slots // 2, 2 * width), F32),
                pltpu.VMEM((nb, nc, nz, slots // 2, 2 * width), F32),
                pltpu.VMEM((nb, rows // 2, 2 * width), BF16),
                pltpu.VMEM((pairs, nc // 2, nz, rows // 2, 2 * width), BF16),
                pltpu.VMEM((pairs, rows // 2, 2 * width), F32),
                pltpu.VMEM((pairs, rows // 2, 2 * width), F32),
                pltpu.VMEM((nb, rows, width), F32),
                pltpu.VMEM((nb, nb, width, width), F32),
                pltpu.VMEM((tall, wide), BF16),
                pltpu.VMEM((tall, wide), BF16),
                pltpu.VMEM((CHUNKS, nz, slots, m // CHUNKS), BF16),
                pltpu.VMEM((CHUNKS, nz, slots, m // CHUNKS), BF16),
                pltpu.VMEM((nz, slots, wide), BF16),
                pltpu.VMEM((nz, slots, wide), BF16),
                pltpu.VMEM((rows, wide), F32),
                pltpu.VMEM((nz - 2, slots, wide), BF16),
                pltpu.VMEM((nz - 2, slots, wide), BF16),
                pltpu.VMEM((slots, m), BF16),
                pltpu.VMEM((slots, m), BF16),
                pltpu.VMEM((rows, tall), BF16),
                pltpu.VMEM((tall, wide), BF16),
                pltpu.SMEM(ranks.shape, jnp.int32),
                dma((2,)), dma((4,)), dma((pairs,)), dma((pairs, 2)),
                dma((nc,)), dma((nz,)),
                dma((pairs, nc)), dma((pairs,)),
                dma((pairs,)), dma((pairs,)),
                dma, dma,
                dma, dma,
                dma((pairs, nc * nz)), dma((nb, nc, nz)),
                dma((nb, nc * nz)), dma((pairs, nc // 2, nz)),
                dma((pairs,)), dma((pairs,)),
                dma, dma,
                dma((CHUNKS, nz - 1)), dma((CHUNKS, nz)),
                dma((nz - 1,)), dma((nz,)),
                dma((2,)), dma((2,)),
            ],
            compiler_params=pltpu.CompilerParams(
                collective_id=0, has_side_effects=True, vmem_limit_bytes=40 * 1024 * 1024
            ),
        )(*arrays)

    in_specs = (
        P("row", "rhs", "col"),
        P("row", "rhs", "col"),
        P("row", "rhs", "col"),
        P("row", None, None, "col"),
        P("row", None, None, "col"),
        P(),
    )
    out_specs = P("row", "rhs", "col")
    return jax.shard_map(body, mesh=mesh, in_specs=in_specs, out_specs=out_specs, check_vma=False)
```

```python
import functools

import jax
import jax.numpy as jnp
from jax import lax
from jax.experimental import pallas as pl
from jax.experimental.pallas import tpu as pltpu
from jax.sharding import PartitionSpec as P

F32 = jnp.float32
BF16 = jnp.bfloat16
TILE = 1024
CHUNKS = 1


def dot(a, b):
    return lax.dot_general(a, b, (((1,), (0,)), ((), ())), preferred_element_type=F32)


def dot_t(a, b):
    return lax.dot_general(a, b, (((1,), (1,)), ((), ())), preferred_element_type=F32)


def fold(value):
    half = value.shape[0] // 2
    return jnp.concatenate([value[:half], value[half:]], axis=1)


def unfold(value):
    half = value.shape[1] // 2
    return jnp.concatenate([value[:, :half], value[:, half:]], axis=0)


def kernel(
    nb, nc, nz, width,
    rhs_ref, guess_ref, inv_ref, left_ref, right_ref, ranks_hbm, out_ref,
    inv, rhs_v, guess_v, right_v, low, x, lf, lv, p_rhs, p_left,
    a_out, a_in, a_own, a_sum, c_out, c_in, n_out, n_in, ns_out, ns_in, p_new, q_new,
    li_out, li_in, s_out, s_in, k_out, k_in, k_all, y_out, y_in, w_out, w_in, coef_v, li_sum, ranks_ref,
    inv_sem, in_sem, own_sem, lv_sem, x_send, x_recv, l_send, l_recv, ls_send, ls_recv, sib_send, sib_recv,
    a_send, a_recv, c_send, c_recv, n_send, n_recv, ns_send, ns_recv, li_send, li_recv, rs_send, rs_recv, k_send, k_recv, y_send, y_recv,
):
    row, col, z = lax.axis_index("row"), lax.axis_index("col"), lax.axis_index("rhs")
    slots, part = low.shape[1:]
    m = inv.shape[2]
    rows = nz * slots
    wide = m // 2
    half = col % 2
    sibling = (row, col + 1 - 2 * half, z)
    diag = col == z
    sent = []

    def remote(src, dst, send, recv, where):
        return pltpu.make_async_remote_copy(
            src_ref=src, dst_ref=dst, send_sem=send, recv_sem=recv,
            device_id=where, device_id_type=pl.DeviceIdType.MESH,
        )

    def start(pred, copies):
        @pl.when(pred)
        def _():
            for copy in copies:
                copy.start()
        sent.append((pred, copies))

    def drain():
        for pred, copies in sent:
            @pl.when(pred)
            def _():
                for copy in copies:
                    copy.wait_send()
        sent.clear()

    around = [(dc, dz) for dz in range(nz) for dc in range(nc)]

    def there(r, dc, dz):
        return (r, lax.rem(col + dc, nc), lax.rem(z + dz, nz))

    barrier = pltpu.get_barrier_semaphore()
    for dc, dz in around[1:]:
        pl.semaphore_signal(barrier, inc=1, device_id=there(row, dc, dz), device_id_type=pl.DeviceIdType.MESH)
    for r in range(1, nb):
        @pl.when(row < r)
        def _():
            for dc, dz in around:
                pl.semaphore_signal(barrier, inc=1, device_id=there(r, dc, dz), device_id_type=pl.DeviceIdType.MESH)
    early = [
        pltpu.make_async_copy(src, dst, in_sem.at[i])
        for i, (src, dst) in enumerate(
            ((rhs_ref.at[0], rhs_v), (guess_ref.at[0], guess_v), (right_ref.at[0], right_v), (ranks_hbm, ranks_ref))
        )
    ]
    for load in early:
        load.start()
    shared = [
        pltpu.make_async_copy(
            left_ref.at[0, lax.rem(row + 1 + q, nb), :, pl.ds(h * part, part)], lv.at[q, h], lv_sem.at[q, h]
        )
        for q in range(nb - 1) for h in range(2)
    ]

    @pl.when(diag)
    def _():
        for load in shared:
            load.start()

    ahead = jnp.where(row < nb - 1, 1 - half, half)
    loads = []
    for order in range(2):
        h = ahead if order == 0 else 1 - ahead
        load = pltpu.make_async_copy(
            inv_ref.at[0, pl.ds(pl.multiple_of(h * part, part), part)], inv.at[h], inv_sem.at[order]
        )
        load.start()
        loads.append(load)

    early[0].wait()
    for h in range(2):
        low[h] = rhs_v[:, h * part:(h + 1) * part].astype(BF16)
    @pl.when(row > 0)
    def _():
        early[1].wait()
        early[2].wait()
        coef = dot_t(guess_v[...].astype(BF16), right_v[...].reshape(nb * width, m))
        for i in range(nb - 1):
            c_out[i] = fold(coef[:, i * width:(i + 1) * width])

    pl.semaphore_wait(barrier, nc * nz - 1 + row * (nc * nz))

    def send_left(pred):
        copies = []
        for q in range(nb - 1):
            for k in range(1, nc):
                c = lax.rem(col + k, nc)
                h = lax.rem(c, 2)
                copies.append(
                    remote(lv.at[q, h], lf.at[q, h], l_send.at[q, k], l_recv.at[q], (row, c, z))
                )

        @pl.when(pred & diag)
        def _():
            for load in shared:
                load.wait()

        start(pred & diag, copies)

    send_left(row > 0)
    for i in range(nb - 1):
        start(row > i, [
            remote(c_out.at[i], c_in.at[row, col, z], c_send.at[i, k], c_recv.at[row, col, z], there(i, dc, dz))
            for k, (dc, dz) in enumerate(around)
        ])

    mine = pl.ds(pl.multiple_of(z * slots, slots), slots)

    def send_x(pred):
        copies = []
        for k in range(nc):
            c = lax.rem(col + k, nc)
            h = lax.rem(c, 2)
            copies.append(remote(low.at[h], x.at[h, mine], x_send.at[k], x_recv.at[z], (row, c, col)))
        start(pred, copies[1:])
        start(pred & jnp.logical_not(diag), copies[:1])

    def own(q):
        return pltpu.make_async_copy(
            left_ref.at[0, lax.rem(row + 1 + q, nb), :, pl.ds(pl.multiple_of(half * part, part), part)],
            lf.at[q, half], own_sem.at[q],
        )

    send_x(row == 0)
    send_left(row == 0)
    send_x(row > 0)

    @pl.when(row == 0)
    def _():
        early[1].wait()
        early[2].wait()

    early[3].wait()

    @pl.when(diag)
    def _():
        for q in range(nb - 1):
            own(q).start()
        x[half, mine] = low[half]

    def wait_left(q):
        @pl.when(diag)
        def _():
            own(q).wait()

        @pl.when(jnp.logical_not(diag))
        def _():
            spot = lf.at[q, half]
            remote(spot, spot, l_send.at[0, 0], l_recv.at[q], sibling).wait_recv()

    def wait_x():
        for zz in range(nz):
            @pl.when(jnp.logical_not(diag & (z == zz)))
            def _():
                spot = x.at[half, pl.ds(zz * slots, slots)]
                remote(spot, spot, x_send.at[0], x_recv.at[zz], sibling).wait_recv()

    def send_new(t, i):
        start(row == t, [
            remote(n_out.at[i], n_in.at[t, col // 2, z], n_send.at[i, k], n_recv.at[t, col // 2, z], there(i, dc, dz))
            for k, (dc, dz) in enumerate(around) if dc % 2 == 0
        ])

    strip = part // 4
    for t in range(nb - 1):
        later = nb - 1 - t

        @pl.when(row == t)
        def _():
            span = pl.ds(0, later)
            swap = remote(a_out.at[span], a_in.at[span], a_send, a_recv, sibling)
            loads[0].wait()

            def theirs(i, _):
                cut = pl.ds(pl.multiple_of(i * strip, strip), strip)
                for b in range(later):
                    a_out[b, cut] = dot_t(inv[1 - half, cut], right_v[t + 1 + b]).astype(BF16)
                return _

            lax.fori_loop(0, part // strip, theirs, 0)
            swap.start()
            loads[1].wait()

            def kept(i, _):
                cut = pl.ds(pl.multiple_of(i * strip, strip), strip)
                for b in range(later):
                    a_own[b, cut] = dot_t(inv[half, cut], right_v[t + 1 + b])
                return _

            lax.fori_loop(0, part // strip, kept, 0)
            swap.wait()
            for b in range(later):
                a_sum[b] = (a_own[b] + a_in[b].astype(F32)).astype(BF16)

    def paired(t):
        span = pl.ds(0, t * width)
        return remote(li_out.at[span], li_in.at[span], li_send, li_recv, (row, col, z + 1 - 2 * lax.rem(z, 2)))

    def columns(which, i=0, size=wide):
        return pl.ds(pl.multiple_of(which * wide + i * size, size), size)

    ours = lax.rem(z, 2)

    for t in range(1, nb):
        later = nb - 1 - t
        tall = t * width

        @pl.when(row == t)
        def _():
            swaps = []
            for q in range(later, nb - 1):
                wait_left(q)
                spot = lf.at[q, half]
                copy = remote(spot, spot, ls_send.at[q], ls_recv.at[q], sibling)
                copy.start()
                swaps.append(copy)
            if not later:
                loads[0].wait()

            def first(i, _):
                cut = pl.ds(pl.multiple_of(i * TILE, TILE), TILE)
                p_left[:tall, cut] = dot(lf[later:, half].reshape(tall, part), inv[half, :, cut])
                return _

            lax.fori_loop(0, m // TILE, first, 0)
            if not later:
                loads[1].wait()
            for copy in swaps:
                copy.wait_recv()

            def second(i, _):
                cut = columns(1 - ours, i, TILE)
                value = p_left[:tall, cut] + dot(lf[later:, 1 - half].reshape(tall, part), inv[1 - half, :, cut])
                li_out[:tall, pl.ds(pl.multiple_of(i * TILE, TILE), TILE)] = value.astype(BF16)
                return _

            def third(i, _):
                cut = columns(ours, i, TILE)
                p_left[:tall, cut] += dot(lf[later:, 1 - half].reshape(tall, part), inv[1 - half, :, cut])
                return _

            lax.fori_loop(0, wide // TILE, second, 0)
            paired(t).start()
            lax.fori_loop(0, wide // TILE, third, 0)
            for copy in swaps:
                copy.wait_send()

    swap = remote(x.at[half], x.at[half], sib_send, sib_recv, sibling)
    for t in range(nb):
        later = nb - 1 - t

        @pl.when(row == t)
        def _():
            if later:
                blocks = []
                for j in range(t + 1, nb):
                    parts = []
                    for zz in range(nz):
                        total = None
                        for c in range(nc):
                            spot = c_in.at[j, c, zz]
                            remote(spot, spot, c_send.at[0, 0], c_recv.at[j, c, zz], sibling).wait_recv()
                            term = c_in[j, c, zz]
                            total = term if total is None else total + term
                        parts.append(unfold(total))
                    whole = jnp.concatenate(parts, axis=0)
                    lane = lax.broadcasted_iota(jnp.int32, whole.shape, 1)
                    blocks.append(jnp.where(lane < ranks_ref[t, j], whole, jnp.zeros_like(whole)).astype(BF16))
                coefs = blocks[0] if later == 1 else jnp.concatenate(blocks, axis=1)
                for q in range(later):
                    wait_left(q)
            wait_x()
            if later:
                coupled = dot(coefs, lf[:later, half].reshape(later * width, part))
                rest = (x[half].astype(F32) - coupled).astype(BF16)
                x[half] = rest
            swap.start()
            if later:
                for i in range(t + 1, nb):
                    share = dot(rest, a_sum[i - t - 1])
                    if t:
                        p_new[i] = share
                        for j in range(t):
                            q_new[i, j] = dot(lf[later + j, half], a_sum[i - t - 1])
                    else:
                        n_out[i] = fold(share).astype(BF16)

    for i in range(1, nb):
        send_new(0, i)

    @pl.when(row > 0)
    def _():
        def first(i, _):
            cut = pl.ds(pl.multiple_of(i * TILE, TILE), TILE)
            p_rhs[:, cut] = dot(x[half], inv[half, :, cut])
            return _

        lax.fori_loop(0, m // TILE, first, 0)

    far = x.at[1 - half]
    remote(far, far, sib_send, sib_recv, sibling).wait_recv()

    span_m = m // CHUNKS
    partner = z + 1 - 2 * ours
    beyond = [lax.rem(z - ours + 2 * step + e, nz) for step in range(1, nz // 2) for e in range(2)]
    others = beyond + [partner]

    def pieces(ch):
        return [
            remote(
                s_out.at[ch, other], s_in.at[ch, z], rs_send.at[ch, i], rs_recv.at[ch, z], (row, col, other)
            )
            for i, other in enumerate(others)
        ]

    def across(i, other):
        return remote(k_out.at[other], k_in.at[z], k_send.at[i], k_recv.at[z], (row, col, other))

    partner = z + 1 - 2 * ours
    beyond = [lax.rem(z - ours + 2 * step + e, nz) for step in range(1, nz // 2) for e in range(2)]
    outer = remote(y_out, y_in, y_send.at[0], y_recv.at[0], (row, col, partner))
    inner = remote(w_out, w_in, y_send.at[1], y_recv.at[1], (row, col, partner))

    def block(which):
        return pl.ds(pl.multiple_of(which * slots, slots), slots)

    def second(which):
        def tile(i, _):
            cut = columns(which, i, TILE)
            p_rhs[:, cut] += dot(x[1 - half], inv[1 - half, :, cut])
            return _

        lax.fori_loop(0, wide // TILE, tile, 0)

    @pl.when(row == 0)
    def _():
        for ch in range(CHUNKS):
            def tile(i, _):
                at = pl.ds(pl.multiple_of(i * TILE, TILE), TILE)
                cut = pl.ds(pl.multiple_of(ch * span_m + i * TILE, TILE), TILE)
                now = dot(x[half], inv[half, :, cut]) + dot(x[1 - half], inv[1 - half, :, cut])
                p_rhs[:, cut] = now
                for zz in range(nz):
                    s_out[ch, zz, :, at] = now[zz * slots:(zz + 1) * slots].astype(BF16)
                return _

            lax.fori_loop(0, span_m // TILE, tile, 0)
            for copy in pieces(ch):
                copy.start()

    @pl.when(row > 0)
    def _():
        second(1 - ours)
        for k, other in enumerate(beyond):
            y_out[k] = p_rhs[block(other), columns(1 - ours)].astype(BF16)
        outer.start()
        second(ours)
        w_out[...] = p_rhs[block(partner)].astype(BF16)
        inner.start()

    swap.wait_send()
    drain()

    for t in range(1, nb):
        later = nb - 1 - t
        tall = t * width

        @pl.when(row == t)
        def _():
            blocks = []
            for j in range(t):
                total = None
                for c in range(nc // 2):
                    for zz in range(nz):
                        spot = n_in.at[j, c, zz]
                        remote(spot, spot, n_send.at[0, 0], n_recv.at[j, c, zz], sibling).wait_recv()
                        term = n_in[j, c, zz].astype(F32)
                        total = term if total is None else total + term
                ns_out[j] = total
                other_half = remote(ns_out.at[j], ns_in.at[j], ns_send.at[j], ns_recv.at[j], sibling)
                other_half.start()
                if j == t - 1:
                    paired(t).wait_recv()
                    li_sum[:tall] = (p_left[:tall, columns(ours)] + li_in[:tall].astype(F32)).astype(BF16)
                other_half.wait()
                total = total + ns_in[j]
                whole = unfold(total)
                lane = lax.broadcasted_iota(jnp.int32, whole.shape, 1)
                blocks.append(jnp.where(lane < ranks_ref[t, j], whole, jnp.zeros_like(whole)).astype(BF16))
            for i in range(t + 1, nb):
                share = p_new[i]
                for j in range(t):
                    share = share - dot(blocks[j], q_new[i, j].astype(BF16))
                n_out[i] = fold(share).astype(BF16)
            coefs = blocks[0] if t == 1 else jnp.concatenate(blocks, axis=1)
            coef_v[:, :tall] = coefs

        for i in range(t + 1, nb):
            send_new(t, i)

        @pl.when(row == t)
        def _():
            k_all[...] = dot(coef_v[:, :tall], li_sum[:tall])
            outer.wait_recv()
            for k, other in enumerate(beyond):
                value = p_rhs[block(other), columns(ours)] + y_in[k].astype(F32) - k_all[block(other)]
                k_out[other] = value.astype(BF16)
                across(k, other).start()
            k_out[partner] = (-k_all[block(partner)]).astype(BF16)
            across(nz - 2, partner).start()

    @pl.when(row == 0)
    def _():
        for ch in range(CHUNKS):
            cut = slice(ch * span_m, (ch + 1) * span_m)
            total = p_rhs[mine, cut]
            for other in others:
                spot = s_in.at[ch, other]
                remote(spot, spot, rs_send.at[0, 0], rs_recv.at[ch, other], (row, col, other)).wait_recv()
                total = total + s_in[ch, other].astype(F32)
            out_ref[0, :, cut] = total
        for ch in range(CHUNKS):
            for copy in pieces(ch):
                copy.wait_send()

    @pl.when(row > 0)
    def _():
        inner.wait_recv()
        p_rhs[mine, columns(ours)] -= k_all[mine]
        total = p_rhs[mine] + w_in[...].astype(F32)
        out_ref[0] = total
        for other in [partner] + beyond:
            spot = k_in.at[other]
            remote(spot, spot, k_send.at[0], k_recv.at[other], (row, col, other)).wait_recv()
            cut = columns(lax.rem(other, 2))
            out_ref[0, :, cut] = out_ref[0, :, cut] + k_in[other].astype(F32)
        for k, other in enumerate(beyond + [partner]):
            across(k, other).wait_send()
        outer.wait_send()
        inner.wait_send()

    for t in range(1, nb):
        @pl.when(row == t)
        def _():
            paired(t).wait_send()
    drain()


def solution(mesh):
    nb, nc, nz = mesh.shape["row"], mesh.shape["col"], mesh.shape["rhs"]

    def body(right_side, guess, inverse, left_factor, right_factor, ranks):
        slots, m = right_side.shape[1:]
        width = left_factor.shape[2]
        rows = nz * slots
        part = inverse.shape[1] // 2
        pairs = nb - 1
        tall = pairs * width
        wide = m // 2
        dma = pltpu.SemaphoreType.DMA
        hbm = pl.BlockSpec(memory_space=pltpu.HBM)
        vmem = pl.BlockSpec(memory_space=pltpu.VMEM)
        arrays = [
            pltpu.with_memory_space_constraint(array, pltpu.HBM)
            for array in (right_side, guess, inverse, left_factor, right_factor, ranks)
        ]
        return pl.pallas_call(
            functools.partial(kernel, nb, nc, nz, width),
            out_shape=jax.ShapeDtypeStruct(right_side.shape, F32),
            in_specs=[
                hbm, hbm, hbm, hbm, hbm,
                hbm,
            ],
            out_specs=vmem,
            scratch_shapes=[
                pltpu.VMEM((2, part, m), BF16),
                pltpu.VMEM((slots, m), F32),
                pltpu.VMEM((slots, m), F32),
                pltpu.VMEM((nb, width, m), BF16),
                pltpu.VMEM((2, slots, part), BF16),
                pltpu.VMEM((2, rows, part), BF16),
                pltpu.VMEM((pairs, 2, width, part), BF16),
                pltpu.VMEM((pairs, 2, width, part), BF16),
                pltpu.VMEM((rows, m), F32),
                pltpu.VMEM((tall, m), F32),
                pltpu.VMEM((pairs, part, width), BF16),
                pltpu.VMEM((pairs, part, width), BF16),
                pltpu.VMEM((pairs, part, width), F32),
                pltpu.VMEM((pairs, part, width), BF16),
                pltpu.VMEM((pairs, slots // 2, 2 * width), F32),
                pltpu.VMEM((nb, nc, nz, slots // 2, 2 * width), F32),
                pltpu.VMEM((nb, rows // 2, 2 * width), BF16),
                pltpu.VMEM((pairs, nc // 2, nz, rows // 2, 2 * width), BF16),
                pltpu.VMEM((pairs, rows // 2, 2 * width), F32),
                pltpu.VMEM((pairs, rows // 2, 2 * width), F32),
                pltpu.VMEM((nb, rows, width), F32),
                pltpu.VMEM((nb, nb, width, width), F32),
                pltpu.VMEM((tall, wide), BF16),
                pltpu.VMEM((tall, wide), BF16),
                pltpu.VMEM((CHUNKS, nz, slots, m // CHUNKS), BF16),
                pltpu.VMEM((CHUNKS, nz, slots, m // CHUNKS), BF16),
                pltpu.VMEM((nz, slots, wide), BF16),
                pltpu.VMEM((nz, slots, wide), BF16),
                pltpu.VMEM((rows, wide), F32),
                pltpu.VMEM((nz - 2, slots, wide), BF16),
                pltpu.VMEM((nz - 2, slots, wide), BF16),
                pltpu.VMEM((slots, m), BF16),
                pltpu.VMEM((slots, m), BF16),
                pltpu.VMEM((rows, tall), BF16),
                pltpu.VMEM((tall, wide), BF16),
                pltpu.SMEM(ranks.shape, jnp.int32),
                dma((2,)), dma((4,)), dma((pairs,)), dma((pairs, 2)),
                dma((nc,)), dma((nz,)),
                dma((pairs, nc)), dma((pairs,)),
                dma((pairs,)), dma((pairs,)),
                dma, dma,
                dma, dma,
                dma((pairs, nc * nz)), dma((nb, nc, nz)),
                dma((nb, nc * nz)), dma((pairs, nc // 2, nz)),
                dma((pairs,)), dma((pairs,)),
                dma, dma,
                dma((CHUNKS, nz - 1)), dma((CHUNKS, nz)),
                dma((nz - 1,)), dma((nz,)),
                dma((2,)), dma((2,)),
            ],
            compiler_params=pltpu.CompilerParams(
                collective_id=0, has_side_effects=True, vmem_limit_bytes=40 * 1024 * 1024
            ),
        )(*arrays)

    in_specs = (
        P("row", "rhs", "col"),
        P("row", "rhs", "col"),
        P("row", "rhs", "col"),
        P("row", None, None, "col"),
        P("row", None, None, "col"),
        P(),
    )
    out_specs = P("row", "rhs", "col")
    return jax.shard_map(body, mesh=mesh, in_specs=in_specs, out_specs=out_specs, check_vma=False)
```

```python
import functools

import jax
import jax.numpy as jnp
from jax import lax
from jax.experimental import pallas as pl
from jax.experimental.pallas import tpu as pltpu
from jax.sharding import PartitionSpec as P

F32 = jnp.float32
BF16 = jnp.bfloat16
TILE = 1024
CHUNKS = 1


def dot(a, b):
    return lax.dot_general(a, b, (((1,), (0,)), ((), ())), preferred_element_type=F32)


def dot_t(a, b):
    return lax.dot_general(a, b, (((1,), (1,)), ((), ())), preferred_element_type=F32)


def fold(value):
    half = value.shape[0] // 2
    return jnp.concatenate([value[:half], value[half:]], axis=1)


def unfold(value):
    half = value.shape[1] // 2
    return jnp.concatenate([value[:, :half], value[:, half:]], axis=0)


def kernel(
    nb, nc, nz, width,
    rhs_ref, guess_ref, inv_ref, left_ref, right_ref, ranks_hbm, out_ref,
    inv, rhs_v, guess_v, right_v, low, x, lf, lv, p_rhs, p_left,
    a_out, a_in, a_own, a_sum, c_out, c_in, n_out, n_in, ns_out, ns_in, p_new, q_new,
    li_out, li_in, s_out, s_in, k_out, k_in, k_all, y_out, y_in, w_out, w_in, coef_v, li_sum, ranks_ref,
    inv_sem, in_sem, own_sem, lv_sem, x_send, x_recv, l_send, l_recv, ls_send, ls_recv, sib_send, sib_recv,
    a_send, a_recv, c_send, c_recv, n_send, n_recv, ns_send, ns_recv, li_send, li_recv, rs_send, rs_recv, k_send, k_recv, y_send, y_recv,
):
    row, col, z = lax.axis_index("row"), lax.axis_index("col"), lax.axis_index("rhs")
    slots, part = low.shape[1:]
    m = inv.shape[2]
    rows = nz * slots
    wide = m // 2
    half = col % 2
    sibling = (row, col + 1 - 2 * half, z)
    diag = col == z
    sent = []

    def remote(src, dst, send, recv, where):
        return pltpu.make_async_remote_copy(
            src_ref=src, dst_ref=dst, send_sem=send, recv_sem=recv,
            device_id=where, device_id_type=pl.DeviceIdType.MESH,
        )

    def start(pred, copies):
        @pl.when(pred)
        def _():
            for copy in copies:
                copy.start()
        sent.append((pred, copies))

    def drain():
        for pred, copies in sent:
            @pl.when(pred)
            def _():
                for copy in copies:
                    copy.wait_send()
        sent.clear()

    around = [(dc, dz) for dz in range(nz) for dc in range(nc)]

    def there(r, dc, dz):
        return (r, lax.rem(col + dc, nc), lax.rem(z + dz, nz))

    barrier = pltpu.get_barrier_semaphore()
    for dc, dz in around[1:]:
        pl.semaphore_signal(barrier, inc=1, device_id=there(row, dc, dz), device_id_type=pl.DeviceIdType.MESH)
    for r in range(1, nb):
        @pl.when(row < r)
        def _():
            for dc, dz in around:
                pl.semaphore_signal(barrier, inc=1, device_id=there(r, dc, dz), device_id_type=pl.DeviceIdType.MESH)
    early = [
        pltpu.make_async_copy(src, dst, in_sem.at[i])
        for i, (src, dst) in enumerate(
            ((rhs_ref.at[0], rhs_v), (guess_ref.at[0], guess_v), (right_ref.at[0], right_v), (ranks_hbm, ranks_ref))
        )
    ]
    for load in early:
        load.start()
    shared = [
        pltpu.make_async_copy(
            left_ref.at[0, lax.rem(row + 1 + q, nb), :, pl.ds(h * part, part)], lv.at[q, h], lv_sem.at[q, h]
        )
        for q in range(nb - 1) for h in range(2)
    ]

    @pl.when(diag)
    def _():
        for load in shared:
            load.start()

    ahead = jnp.where(row < nb - 1, 1 - half, half)
    loads = []
    for order in range(2):
        h = ahead if order == 0 else 1 - ahead
        load = pltpu.make_async_copy(
            inv_ref.at[0, pl.ds(pl.multiple_of(h * part, part), part)], inv.at[h], inv_sem.at[order]
        )
        load.start()
        loads.append(load)

    early[0].wait()
    for h in range(2):
        low[h] = rhs_v[:, h * part:(h + 1) * part].astype(BF16)
    @pl.when(row > 0)
    def _():
        early[1].wait()
        early[2].wait()
        coef = dot_t(guess_v[...].astype(BF16), right_v[...].reshape(nb * width, m))
        for i in range(nb - 1):
            c_out[i] = fold(coef[:, i * width:(i + 1) * width])

    pl.semaphore_wait(barrier, nc * nz - 1 + row * (nc * nz))

    def send_left(pred):
        copies = []
        for q in range(nb - 1):
            for k in range(1, nc):
                c = lax.rem(col + k, nc)
                h = lax.rem(c, 2)
                copies.append(
                    remote(lv.at[q, h], lf.at[q, h], l_send.at[q, k], l_recv.at[q], (row, c, z))
                )

        @pl.when(pred & diag)
        def _():
            for load in shared:
                load.wait()

        start(pred & diag, copies)

    send_left(row > 0)
    for i in range(nb - 1):
        start(row > i, [
            remote(c_out.at[i], c_in.at[row, col, z], c_send.at[i, k], c_recv.at[row, col, z], there(i, dc, dz))
            for k, (dc, dz) in enumerate(around)
        ])

    mine = pl.ds(pl.multiple_of(z * slots, slots), slots)

    def send_x(pred):
        copies = []
        for k in range(nc):
            c = lax.rem(col + k, nc)
            h = lax.rem(c, 2)
            copies.append(remote(low.at[h], x.at[h, mine], x_send.at[k], x_recv.at[z], (row, c, col)))
        start(pred & jnp.logical_not(diag), copies[:1])
        start(pred, copies[1:])

    def own(q):
        return pltpu.make_async_copy(
            left_ref.at[0, lax.rem(row + 1 + q, nb), :, pl.ds(pl.multiple_of(half * part, part), part)],
            lf.at[q, half], own_sem.at[q],
        )

    send_x(row == 0)
    send_left(row == 0)
    send_x(row > 0)

    @pl.when(row == 0)
    def _():
        early[1].wait()
        early[2].wait()

    early[3].wait()

    @pl.when(diag)
    def _():
        for q in range(nb - 1):
            own(q).start()
        x[half, mine] = low[half]

    def wait_left(q):
        @pl.when(diag)
        def _():
            own(q).wait()

        @pl.when(jnp.logical_not(diag))
        def _():
            spot = lf.at[q, half]
            remote(spot, spot, l_send.at[0, 0], l_recv.at[q], sibling).wait_recv()

    def wait_x():
        for zz in range(nz):
            @pl.when(jnp.logical_not(diag & (z == zz)))
            def _():
                spot = x.at[half, pl.ds(zz * slots, slots)]
                remote(spot, spot, x_send.at[0], x_recv.at[zz], sibling).wait_recv()

    def send_new(t, i):
        start(row == t, [
            remote(n_out.at[i], n_in.at[t, col // 2, z], n_send.at[i, k], n_recv.at[t, col // 2, z], there(i, dc, dz))
            for k, (dc, dz) in enumerate(around) if dc % 2 == 0
        ])

    strip = part // 4
    for t in range(nb - 1):
        later = nb - 1 - t

        @pl.when(row == t)
        def _():
            span = pl.ds(0, later)
            swap = remote(a_out.at[span], a_in.at[span], a_send, a_recv, sibling)
            loads[0].wait()

            def theirs(i, _):
                cut = pl.ds(pl.multiple_of(i * strip, strip), strip)
                for b in range(later):
                    a_out[b, cut] = dot_t(inv[1 - half, cut], right_v[t + 1 + b]).astype(BF16)
                return _

            lax.fori_loop(0, part // strip, theirs, 0)
            swap.start()
            loads[1].wait()

            def kept(i, _):
                cut = pl.ds(pl.multiple_of(i * strip, strip), strip)
                for b in range(later):
                    a_own[b, cut] = dot_t(inv[half, cut], right_v[t + 1 + b])
                return _

            lax.fori_loop(0, part // strip, kept, 0)
            swap.wait()
            for b in range(later):
                a_sum[b] = (a_own[b] + a_in[b].astype(F32)).astype(BF16)

    def paired(t):
        span = pl.ds(0, t * width)
        return remote(li_out.at[span], li_in.at[span], li_send, li_recv, (row, col, z + 1 - 2 * lax.rem(z, 2)))

    def columns(which, i=0, size=wide):
        return pl.ds(pl.multiple_of(which * wide + i * size, size), size)

    ours = lax.rem(z, 2)

    for t in range(1, nb):
        later = nb - 1 - t
        tall = t * width

        @pl.when(row == t)
        def _():
            swaps = []
            for q in range(later, nb - 1):
                wait_left(q)
                spot = lf.at[q, half]
                copy = remote(spot, spot, ls_send.at[q], ls_recv.at[q], sibling)
                copy.start()
                swaps.append(copy)
            if not later:
                loads[0].wait()

            def first(i, _):
                cut = pl.ds(pl.multiple_of(i * TILE, TILE), TILE)
                p_left[:tall, cut] = dot(lf[later:, half].reshape(tall, part), inv[half, :, cut])
                return _

            lax.fori_loop(0, m // TILE, first, 0)
            if not later:
                loads[1].wait()
            for copy in swaps:
                copy.wait_recv()

            def second(i, _):
                cut = columns(1 - ours, i, TILE)
                value = p_left[:tall, cut] + dot(lf[later:, 1 - half].reshape(tall, part), inv[1 - half, :, cut])
                li_out[:tall, pl.ds(pl.multiple_of(i * TILE, TILE), TILE)] = value.astype(BF16)
                return _

            def third(i, _):
                cut = columns(ours, i, TILE)
                p_left[:tall, cut] += dot(lf[later:, 1 - half].reshape(tall, part), inv[1 - half, :, cut])
                return _

            lax.fori_loop(0, wide // TILE, second, 0)
            paired(t).start()
            lax.fori_loop(0, wide // TILE, third, 0)
            for copy in swaps:
                copy.wait_send()

    swap = remote(x.at[half], x.at[half], sib_send, sib_recv, sibling)
    for t in range(nb):
        later = nb - 1 - t

        @pl.when(row == t)
        def _():
            if later:
                blocks = []
                for j in range(t + 1, nb):
                    parts = []
                    for zz in range(nz):
                        total = None
                        for c in range(nc):
                            spot = c_in.at[j, c, zz]
                            remote(spot, spot, c_send.at[0, 0], c_recv.at[j, c, zz], sibling).wait_recv()
                            term = c_in[j, c, zz]
                            total = term if total is None else total + term
                        parts.append(unfold(total))
                    whole = jnp.concatenate(parts, axis=0)
                    lane = lax.broadcasted_iota(jnp.int32, whole.shape, 1)
                    blocks.append(jnp.where(lane < ranks_ref[t, j], whole, jnp.zeros_like(whole)).astype(BF16))
                coefs = blocks[0] if later == 1 else jnp.concatenate(blocks, axis=1)
                for q in range(later):
                    wait_left(q)
            wait_x()
            if later:
                coupled = dot(coefs, lf[:later, half].reshape(later * width, part))
                rest = (x[half].astype(F32) - coupled).astype(BF16)
                x[half] = rest
            swap.start()
            if later:
                for i in range(t + 1, nb):
                    share = dot(rest, a_sum[i - t - 1])
                    if t:
                        p_new[i] = share
                        for j in range(t):
                            q_new[i, j] = dot(lf[later + j, half], a_sum[i - t - 1])
                    else:
                        n_out[i] = fold(share).astype(BF16)

    for i in range(1, nb):
        send_new(0, i)

    @pl.when(row > 0)
    def _():
        def first(i, _):
            cut = pl.ds(pl.multiple_of(i * TILE, TILE), TILE)
            p_rhs[:, cut] = dot(x[half], inv[half, :, cut])
            return _

        lax.fori_loop(0, m // TILE, first, 0)

    far = x.at[1 - half]
    remote(far, far, sib_send, sib_recv, sibling).wait_recv()

    span_m = m // CHUNKS
    partner = z + 1 - 2 * ours
    beyond = [lax.rem(z - ours + 2 * step + e, nz) for step in range(1, nz // 2) for e in range(2)]
    others = beyond + [partner]

    def pieces(ch):
        return [
            remote(
                s_out.at[ch, other], s_in.at[ch, z], rs_send.at[ch, i], rs_recv.at[ch, z], (row, col, other)
            )
            for i, other in enumerate(others)
        ]

    def across(i, other):
        return remote(k_out.at[other], k_in.at[z], k_send.at[i], k_recv.at[z], (row, col, other))

    partner = z + 1 - 2 * ours
    beyond = [lax.rem(z - ours + 2 * step + e, nz) for step in range(1, nz // 2) for e in range(2)]
    outer = remote(y_out, y_in, y_send.at[0], y_recv.at[0], (row, col, partner))
    inner = remote(w_out, w_in, y_send.at[1], y_recv.at[1], (row, col, partner))

    def block(which):
        return pl.ds(pl.multiple_of(which * slots, slots), slots)

    def second(which):
        def tile(i, _):
            cut = columns(which, i, TILE)
            p_rhs[:, cut] += dot(x[1 - half], inv[1 - half, :, cut])
            return _

        lax.fori_loop(0, wide // TILE, tile, 0)

    @pl.when(row == 0)
    def _():
        for ch in range(CHUNKS):
            def tile(i, _):
                at = pl.ds(pl.multiple_of(i * TILE, TILE), TILE)
                cut = pl.ds(pl.multiple_of(ch * span_m + i * TILE, TILE), TILE)
                now = dot(x[half], inv[half, :, cut]) + dot(x[1 - half], inv[1 - half, :, cut])
                p_rhs[:, cut] = now
                for zz in range(nz):
                    s_out[ch, zz, :, at] = now[zz * slots:(zz + 1) * slots].astype(BF16)
                return _

            lax.fori_loop(0, span_m // TILE, tile, 0)
            for copy in pieces(ch):
                copy.start()

    @pl.when(row > 0)
    def _():
        second(1 - ours)
        for k, other in enumerate(beyond):
            y_out[k] = p_rhs[block(other), columns(1 - ours)].astype(BF16)
        outer.start()
        second(ours)
        w_out[...] = p_rhs[block(partner)].astype(BF16)
        inner.start()

    swap.wait_send()
    drain()

    for t in range(1, nb):
        later = nb - 1 - t
        tall = t * width

        @pl.when(row == t)
        def _():
            paired(t).wait_recv()
            li_sum[:tall] = (p_left[:tall, columns(ours)] + li_in[:tall].astype(F32)).astype(BF16)
            blocks = []
            for j in range(t):
                total = None
                for c in range(nc // 2):
                    for zz in range(nz):
                        spot = n_in.at[j, c, zz]
                        remote(spot, spot, n_send.at[0, 0], n_recv.at[j, c, zz], sibling).wait_recv()
                        term = n_in[j, c, zz].astype(F32)
                        total = term if total is None else total + term
                ns_out[j] = total
                other_half = remote(ns_out.at[j], ns_in.at[j], ns_send.at[j], ns_recv.at[j], sibling)
                other_half.start()
                other_half.wait()
                total = total + ns_in[j]
                whole = unfold(total)
                lane = lax.broadcasted_iota(jnp.int32, whole.shape, 1)
                blocks.append(jnp.where(lane < ranks_ref[t, j], whole, jnp.zeros_like(whole)).astype(BF16))
            for i in range(t + 1, nb):
                share = p_new[i]
                for j in range(t):
                    share = share - dot(blocks[j], q_new[i, j].astype(BF16))
                n_out[i] = fold(share).astype(BF16)
            coefs = blocks[0] if t == 1 else jnp.concatenate(blocks, axis=1)
            coef_v[:, :tall] = coefs

        for i in range(t + 1, nb):
            send_new(t, i)

        @pl.when(row == t)
        def _():
            k_all[...] = dot(coef_v[:, :tall], li_sum[:tall])
            outer.wait_recv()
            for k, other in enumerate(beyond):
                value = p_rhs[block(other), columns(ours)] + y_in[k].astype(F32) - k_all[block(other)]
                k_out[other] = value.astype(BF16)
                across(k, other).start()
            k_out[partner] = (-k_all[block(partner)]).astype(BF16)
            across(nz - 2, partner).start()

    @pl.when(row == 0)
    def _():
        for ch in range(CHUNKS):
            cut = slice(ch * span_m, (ch + 1) * span_m)
            total = p_rhs[mine, cut]
            for other in others:
                spot = s_in.at[ch, other]
                remote(spot, spot, rs_send.at[0, 0], rs_recv.at[ch, other], (row, col, other)).wait_recv()
                total = total + s_in[ch, other].astype(F32)
            out_ref[0, :, cut] = total
        for ch in range(CHUNKS):
            for copy in pieces(ch):
                copy.wait_send()

    @pl.when(row > 0)
    def _():
        inner.wait_recv()
        p_rhs[mine, columns(ours)] -= k_all[mine]
        total = p_rhs[mine] + w_in[...].astype(F32)
        out_ref[0] = total
        for other in [partner] + beyond:
            spot = k_in.at[other]
            remote(spot, spot, k_send.at[0], k_recv.at[other], (row, col, other)).wait_recv()
            cut = columns(lax.rem(other, 2))
            out_ref[0, :, cut] = out_ref[0, :, cut] + k_in[other].astype(F32)
        for k, other in enumerate(beyond + [partner]):
            across(k, other).wait_send()
        outer.wait_send()
        inner.wait_send()

    for t in range(1, nb):
        @pl.when(row == t)
        def _():
            paired(t).wait_send()
    drain()


def solution(mesh):
    nb, nc, nz = mesh.shape["row"], mesh.shape["col"], mesh.shape["rhs"]

    def body(right_side, guess, inverse, left_factor, right_factor, ranks):
        slots, m = right_side.shape[1:]
        width = left_factor.shape[2]
        rows = nz * slots
        part = inverse.shape[1] // 2
        pairs = nb - 1
        tall = pairs * width
        wide = m // 2
        dma = pltpu.SemaphoreType.DMA
        hbm = pl.BlockSpec(memory_space=pltpu.HBM)
        vmem = pl.BlockSpec(memory_space=pltpu.VMEM)
        arrays = [
            pltpu.with_memory_space_constraint(array, pltpu.HBM)
            for array in (right_side, guess, inverse, left_factor, right_factor, ranks)
        ]
        return pl.pallas_call(
            functools.partial(kernel, nb, nc, nz, width),
            out_shape=jax.ShapeDtypeStruct(right_side.shape, F32),
            in_specs=[
                hbm, hbm, hbm, hbm, hbm,
                hbm,
            ],
            out_specs=vmem,
            scratch_shapes=[
                pltpu.VMEM((2, part, m), BF16),
                pltpu.VMEM((slots, m), F32),
                pltpu.VMEM((slots, m), F32),
                pltpu.VMEM((nb, width, m), BF16),
                pltpu.VMEM((2, slots, part), BF16),
                pltpu.VMEM((2, rows, part), BF16),
                pltpu.VMEM((pairs, 2, width, part), BF16),
                pltpu.VMEM((pairs, 2, width, part), BF16),
                pltpu.VMEM((rows, m), F32),
                pltpu.VMEM((tall, m), F32),
                pltpu.VMEM((pairs, part, width), BF16),
                pltpu.VMEM((pairs, part, width), BF16),
                pltpu.VMEM((pairs, part, width), F32),
                pltpu.VMEM((pairs, part, width), BF16),
                pltpu.VMEM((pairs, slots // 2, 2 * width), F32),
                pltpu.VMEM((nb, nc, nz, slots // 2, 2 * width), F32),
                pltpu.VMEM((nb, rows // 2, 2 * width), BF16),
                pltpu.VMEM((pairs, nc // 2, nz, rows // 2, 2 * width), BF16),
                pltpu.VMEM((pairs, rows // 2, 2 * width), F32),
                pltpu.VMEM((pairs, rows // 2, 2 * width), F32),
                pltpu.VMEM((nb, rows, width), F32),
                pltpu.VMEM((nb, nb, width, width), F32),
                pltpu.VMEM((tall, wide), BF16),
                pltpu.VMEM((tall, wide), BF16),
                pltpu.VMEM((CHUNKS, nz, slots, m // CHUNKS), BF16),
                pltpu.VMEM((CHUNKS, nz, slots, m // CHUNKS), BF16),
                pltpu.VMEM((nz, slots, wide), BF16),
                pltpu.VMEM((nz, slots, wide), BF16),
                pltpu.VMEM((rows, wide), F32),
                pltpu.VMEM((nz - 2, slots, wide), BF16),
                pltpu.VMEM((nz - 2, slots, wide), BF16),
                pltpu.VMEM((slots, m), BF16),
                pltpu.VMEM((slots, m), BF16),
                pltpu.VMEM((rows, tall), BF16),
                pltpu.VMEM((tall, wide), BF16),
                pltpu.SMEM(ranks.shape, jnp.int32),
                dma((2,)), dma((4,)), dma((pairs,)), dma((pairs, 2)),
                dma((nc,)), dma((nz,)),
                dma((pairs, nc)), dma((pairs,)),
                dma((pairs,)), dma((pairs,)),
                dma, dma,
                dma, dma,
                dma((pairs, nc * nz)), dma((nb, nc, nz)),
                dma((nb, nc * nz)), dma((pairs, nc // 2, nz)),
                dma((pairs,)), dma((pairs,)),
                dma, dma,
                dma((CHUNKS, nz - 1)), dma((CHUNKS, nz)),
                dma((nz - 1,)), dma((nz,)),
                dma((2,)), dma((2,)),
            ],
            compiler_params=pltpu.CompilerParams(
                collective_id=0, has_side_effects=True, vmem_limit_bytes=40 * 1024 * 1024
            ),
        )(*arrays)

    in_specs = (
        P("row", "rhs", "col"),
        P("row", "rhs", "col"),
        P("row", "rhs", "col"),
        P("row", None, None, "col"),
        P("row", None, None, "col"),
        P(),
    )
    out_specs = P("row", "rhs", "col")
    return jax.shard_map(body, mesh=mesh, in_specs=in_specs, out_specs=out_specs, check_vma=False)
```
